32 devices in a mesh: row: 4 (over z), col: 8 (over y, x, core).
Axes of the slice: x: 2, y: 2, z: 4, core: 2. Of those that a mesh axis runs over, the one named last changes fastest.
Arguments:
- level_set: float32 [384, 384, 384], P('col', 'row'), may hold values from -7 to 7
- image: float32 [384, 384, 384], P('col', 'row'), may hold values from -6 to 6
Outputs:
- updated_level: float32 [384, 384, 384], P('col', 'row')
The draws below stay inside these ranges and needn't reach their ends.
All inputs are finite; a program needn't handle non-finite values.
Results may differ from the reference program's by a relative error of at most 0.00021.
Values sent between devices are 32-bit elements; how exact they have to be, the bound alone decides.
No kernel may reach another device: no remote copies, remote signals or barrier semaphores. Data moves between devices by JAX's collectives and lax.ppermute only.
A program may use at most 192 MiB of HBM per device.

```python
import jax
import jax.numpy as jnp

N = 384
RADIUS = 6


def pattern_field(key):
    base = jax.random.fold_in(key, 7)
    wave_numbers = jax.random.randint(jax.random.fold_in(base, 1), (3, 3), 1, 4).astype(jnp.float32)
    phases = jax.random.uniform(jax.random.fold_in(base, 2), (3,), jnp.float32, -3.14159, 3.14159)
    coord_z = jnp.arange(N, dtype=jnp.float32).reshape(N, 1, 1)
    coord_y = jnp.arange(N, dtype=jnp.float32).reshape(1, N, 1)
    coord_x = jnp.arange(N, dtype=jnp.float32).reshape(1, 1, N)
    summed = jnp.zeros((N, N, N), jnp.float32)
    for which in range(3):
        angle = 2.0 * 3.14159265 * (wave_numbers[which, 0] * coord_z + wave_numbers[which, 1] * coord_y + wave_numbers[which, 2] * coord_x) / N + phases[which]
        summed = summed + jnp.cos(angle)
    return summed / 1.2247


def noise_field(key, label, limit):
    noise_key = jax.random.fold_in(key, label)
    return jax.random.truncated_normal(noise_key, -limit, limit, (N, N, N), jnp.float32)


def alternation(key, label):
    base = jax.random.fold_in(key, label)
    strength = 0.35
    sign_draw = jnp.where(jax.random.bernoulli(base, 0.5, (3,)), 1.0, -1.0).astype(jnp.float32)
    parity = (jnp.arange(N, dtype=jnp.int32) % 2).astype(jnp.float32)
    flip_sign = 1.0 - 2.0 * parity
    return strength * (sign_draw[0] * flip_sign.reshape(N, 1, 1) + sign_draw[1] * flip_sign.reshape(1, N, 1) + sign_draw[2] * flip_sign.reshape(1, 1, N))


def draw_level_set(key, part):
    return 0.8 * pattern_field(key) + noise_field(key, 11, 3.9) + alternation(key, 17)


def draw_image(key, part):
    return pattern_field(key) + 0.7 * noise_field(key, 13, 3.5) + alternation(key, 19)


def setup_inputs(seed: int = 0) -> dict:
    seeds = jax.random.split(jax.random.key(seed), 3)
    return {
        "level_set": draw_level_set(jax.random.fold_in(seeds[2], 71), 0),
        "image": draw_image(jax.random.fold_in(seeds[2], 71), 0),
    }


sigma_cells = 8.0
dt_step = 0.5
nu_diff = 0.1
eps_fit = 0.05


def kernel_row(length):
    indices = jnp.arange(length, dtype=jnp.int32)
    distance = jnp.minimum(indices, length - indices)
    spacing = distance.astype(jnp.float32)
    weights = jnp.where(distance <= RADIUS, jnp.exp(-spacing * spacing / (2.0 * sigma_cells * sigma_cells)), 0.0)
    return weights / jnp.sum(weights)


def smooth(volume, kernel_spec):
    for which_axis in range(3):
        spectrum = jnp.fft.rfft(volume, axis=which_axis)
        shape_list = [1, 1, 1]
        shape_list[which_axis] = kernel_spec.shape[0]
        volume = jnp.fft.irfft(spectrum * kernel_spec.reshape(shape_list), n=N, axis=which_axis)
        volume = volume.astype(jnp.float32)
    return volume


def reference(level_set, image):
    heaviside = 0.5 + jnp.arctan(level_set) / jnp.pi
    kernel_spec = jnp.fft.rfft(kernel_row(N))
    first = smooth(heaviside * image, kernel_spec)
    second = smooth(heaviside, kernel_spec)
    third = smooth(image, kernel_spec)
    fourth = smooth(image * image, kernel_spec)
    inside_mean = first / (second + eps_fit)
    outside_mean = (third - first) / (1.0 - second + eps_fit)
    spread = fourth - third * third + eps_fit
    slope_term = 2.0 * (inside_mean - outside_mean) / spread
    offset = (outside_mean * outside_mean - inside_mean * inside_mean) / spread
    forcing = image * slope_term + offset
    laplace = (jnp.roll(level_set, 1, 0) + jnp.roll(level_set, -1, 0)
               + jnp.roll(level_set, 1, 1) + jnp.roll(level_set, -1, 1)
               + jnp.roll(level_set, 1, 2) + jnp.roll(level_set, -1, 2) - 6.0 * level_set)
    dirac_weight = 1.0 / (jnp.pi * (1.0 + level_set * level_set))
    return level_set + dt_step * (nu_diff * laplace + dirac_weight * forcing)
```

```python
import functools
import math

import jax
import jax.numpy as jnp
import numpy as np
from jax import lax
from jax.experimental import pallas as pl
from jax.experimental.pallas import tpu as pltpu
from jax.sharding import PartitionSpec as P

RADIUS = 6
SLAB = 8
EDGE = 8
TILE = 16
LANES = 128

sigma_cells = 8.0
dt_step = 0.5
nu_diff = 0.1
eps_fit = 0.05

ATAN_COEFS = (
    0.318309854, -0.106098923, 0.0635640505, -0.0446161759,
    0.0315320858, -0.0188971351, 0.00769233704, -0.0014861167,
)
TAP_SCALE = 0.519


def taps():
    d = np.arange(RADIUS + 1, dtype=np.float64)
    exact = np.exp(-d * d / (2.0 * sigma_cells * sigma_cells))
    short = np.asarray((TAP_SCALE * exact).astype(np.float32).astype(jnp.bfloat16))
    short64 = short.astype(np.float64)
    short_sum = short64[0] + 2.0 * short64[1:].sum()
    z_taps = exact / (exact[0] + 2.0 * exact[1:].sum()) / (short_sum * short_sum)
    return [float(v) for v in z_taps], short


def band(out_pos, in_pos, period=None):
    _, short = taps()
    dist = np.abs(out_pos[:, None] - in_pos[None, :])
    if period is not None:
        dist = np.minimum(dist, period - dist)
    table = np.where(dist <= RADIUS, short.astype(np.float32)[np.minimum(dist, RADIUS)], 0.0)
    return jnp.asarray(table.astype(np.float32), jnp.bfloat16)


def heaviside(x):
    far = jnp.abs(x) > 1.0
    t = jnp.where(far, 1.0 / x, x)
    z = t * t
    p = ATAN_COEFS[-1]
    for c in ATAN_COEFS[-2::-1]:
        p = p * z + c
    p = p * t
    base = jnp.where(far, jnp.where(x > 0.0, 1.0, 0.0), 0.5)
    return base + jnp.where(far, -p, p)


def part_kernel(plan, *refs):
    n_in = len(plan["inputs"])
    srcs = refs[:n_in]
    wy_ref, wx_ref = refs[n_in], refs[n_in + 1]
    pos = n_in + 2 + (1 if plan["aliased"] else 0)
    out_ref = refs[pos]
    lev, img, hea, zb, xb, xr, ob, in_sem, out_sem = refs[pos + 1 :]
    rows, rows_out, length = plan["rows"], plan["rows_out"], plan["length"]
    groups, slabs = plan["groups"], plan["slabs"]
    z_taps, _ = taps()

    copies = []
    for k, (which, src_index, dst_index) in enumerate(plan["copies"]):
        for f, dst in enumerate((lev, img)):
            src = srcs[which[f]]
            for axis_lead in src_index[f][0]:
                src = src.at[axis_lead]
            src = src.at[tuple(pl.ds(a, n) for a, n in src_index[f][1])]
            copy = pltpu.make_async_copy(
                src, dst.at[tuple(pl.ds(a, n) for a, n in dst_index)], in_sem.at[2 * k + f]
            )
            copy.start()
            copies.append(copy)
    for copy in copies:
        copy.wait()

    def fill(z, carry):
        hea[z] = heaviside(lev[z])
        return carry

    lax.fori_loop(plan["z_used"][0], plan["z_used"][1], fill, 0)

    def slab(s, carry):
        first = plan["slab_start"](s)

        def along_z(r, c):
            at = pl.multiple_of(r * TILE, TILE)
            for lane in range(0, length, LANES):
                for f in range(4):
                    vals = []
                    for z in range(SLAB + 2 * RADIUS):
                        where = (first + z, pl.ds(at, TILE), pl.ds(lane, LANES))
                        if f == 0:
                            v = hea[where] * img[where]
                        elif f == 1:
                            v = hea[where]
                        elif f == 2:
                            v = img[where]
                        else:
                            v = img[where]
                            v = v * v
                        vals.append(v)
                    for z in range(SLAB):
                        acc = vals[z + RADIUS] * z_taps[0]
                        for d in range(1, RADIUS + 1):
                            acc = acc + (vals[z + RADIUS - d] + vals[z + RADIUS + d]) * z_taps[d]
                        hi = acc.astype(jnp.bfloat16)
                        lo = (acc - hi.astype(jnp.float32)).astype(jnp.bfloat16)
                        cols = pl.ds(f * length + lane, LANES)
                        zb[z, pl.ds(at, TILE), cols] = hi
                        zb[z, pl.ds(at + rows, TILE), cols] = lo
            return c

        lax.fori_loop(0, rows // TILE, along_z, 0)

        def along_yx(z, c):
            for f in range(4):
                acc = jnp.dot(
                    wy_ref[...], zb[z, :, f * length : (f + 1) * length],
                    preferred_element_type=jnp.float32,
                )
                hi = acc.astype(jnp.bfloat16)
                lo = (acc - hi.astype(jnp.float32)).astype(jnp.bfloat16)
                xb[f * rows_out : (f + 1) * rows_out, :length] = hi
                xb[f * rows_out : (f + 1) * rows_out, length:] = lo
            xr[...] = jnp.dot(xb[...], wx_ref[...], preferred_element_type=jnp.float32)
            zi = first + RADIUS + z
            row = 0
            for start, count, _ in groups:
                for i in range(0, count, 8):
                    s1, s2, s3, s4 = (
                        xr[f * rows_out + row + i : f * rows_out + row + i + 8, :] for f in range(4)
                    )
                    at = start + i
                    lv = lev[zi, at : at + 8, :]
                    im = img[zi, at : at + 8, :]
                    inner = s2 + eps_fit
                    outer = (1.0 + eps_fit) - s2
                    spread = s4 - s3 * s3 + eps_fit
                    left = s1 * outer
                    right = (s3 - s1) * inner
                    prod = inner * outer
                    denom = (prod * prod) * (spread * (math.pi * (1.0 + lv * lv)))
                    numer = (left - right) * (2.0 * im * prod - (left + right))
                    laplace = (
                        (lev[zi - 1, at : at + 8, :] + lev[zi + 1, at : at + 8, :])
                        + (lev[zi, at - 1 : at + 7, :] + lev[zi, at + 1 : at + 9, :])
                        + (pltpu.roll(lv, 1, 1) + pltpu.roll(lv, length - 1, 1))
                        - 6.0 * lv
                    )
                    ob[s, z, row + i : row + i + 8, :] = lv + dt_step * (
                        nu_diff * laplace + numer / denom
                    )
                row += count
            return c

        lax.fori_loop(0, SLAB, along_yx, 0)
        row = 0
        for g, (_, count, y0) in enumerate(groups):
            pltpu.make_async_copy(
                ob.at[s, :, pl.ds(row, count), :],
                out_ref.at[pl.ds(plan["slab_out"](s), SLAB), pl.ds(y0, count), :],
                out_sem.at[s, g],
            ).start()
            row += count
        return carry

    lax.fori_loop(0, slabs, slab, 0)
    for s in range(slabs):
        row = 0
        for g, (_, count, y0) in enumerate(groups):
            pltpu.make_async_copy(
                ob.at[s, :, pl.ds(row, count), :],
                out_ref.at[pl.ds(plan["slab_out"](s), SLAB), pl.ds(y0, count), :],
                out_sem.at[s, g],
            ).wait()
            row += count


def run_part(plan, shape, srcs, wy, wx, prev):
    rows, rows_out, length, planes = plan["rows"], plan["rows_out"], plan["length"], plan["planes"]
    slabs = plan["slabs"]
    plan = dict(plan, inputs=srcs, aliased=prev is not None)
    any_spec = pl.BlockSpec(memory_space=pl.ANY)
    vmem = pl.BlockSpec(memory_space=pltpu.VMEM)
    args = list(srcs) + [wy, wx] + ([] if prev is None else [prev])
    specs = [any_spec] * len(srcs) + [vmem, vmem] + ([] if prev is None else [any_spec])
    n_out = slabs * SLAB * rows_out * length
    return pl.pallas_call(
        functools.partial(part_kernel, plan),
        out_shape=jax.ShapeDtypeStruct(shape, jnp.float32),
        in_specs=specs,
        out_specs=any_spec,
        scratch_shapes=[
            pltpu.VMEM((planes, rows, length), jnp.float32),
            pltpu.VMEM((planes, rows, length), jnp.float32),
            pltpu.VMEM((planes, rows, length), jnp.float32),
            pltpu.VMEM((SLAB, 2 * rows, 4 * length), jnp.bfloat16),
            pltpu.VMEM((4 * rows_out, 2 * length), jnp.bfloat16),
            pltpu.VMEM((4 * rows_out, length), jnp.float32),
            pltpu.VMEM((slabs, SLAB, rows_out, length), jnp.float32),
            pltpu.SemaphoreType.DMA((2 * len(plan["copies"]),)),
            pltpu.SemaphoreType.DMA((slabs, len(plan["groups"]))),
        ],
        input_output_aliases={} if prev is None else {len(args) - 1: 0},
        compiler_params=pltpu.CompilerParams(vmem_limit_bytes=60 * 1024 * 1024),
        cost_estimate=pl.CostEstimate(
            flops=n_out * 12000, bytes_accessed=n_out * 12, transcendentals=0
        ),
        name=plan["name"],
    )(*args)


def neighbours(axis):
    n = lax.axis_size(axis)
    up = [(i, (i + 1) % n) for i in range(n)]
    return up, [(j, i) for i, j in up]


def body(level_set, image):
    zl, yl, length = level_set.shape
    shape = level_set.shape
    r = RADIUS
    both = jnp.stack([level_set, image])
    y_up, y_down = neighbours("row")
    z_up, z_down = neighbours("col")

    y_before = lax.ppermute(both[:, :, yl - r :, :].transpose(0, 2, 1, 3), "row", y_up)
    y_after = lax.ppermute(both[:, :, :r, :].transpose(0, 2, 1, 3), "row", y_down)
    z_before = lax.ppermute(both[:, zl - r :], "col", z_up)
    z_after = lax.ppermute(both[:, :r], "col", z_down)

    y_rows = np.arange(yl)
    wx1 = band(np.arange(length), np.arange(length), length)
    wx = jnp.concatenate([wx1, wx1], axis=0)

    def doubled(out_pos, in_pos):
        w = band(out_pos, in_pos)
        return jnp.concatenate([w, w], axis=1)

    def block(lead, *ranges):
        return (lead, ranges)

    full = block((), (0, zl), (0, yl), (0, length))
    inner_slabs = (zl - 2 * EDGE) // SLAB
    interior = dict(
        name="interior", rows=yl, rows_out=yl - 2 * EDGE, length=length, planes=zl,
        slabs=inner_slabs, z_used=(EDGE - r, zl - EDGE + r),
        slab_start=lambda s: EDGE - r + SLAB * s, slab_out=lambda s: EDGE + SLAB * s,
        groups=((EDGE, yl - 2 * EDGE, EDGE),),
        copies=[((0, 1), (full, full), full[1])],
    )
    out = run_part(
        interior, shape, [level_set, image],
        doubled(y_rows[EDGE : yl - EDGE], y_rows), wx, None,
    )

    edge_last = jnp.stack([y_before[:, :, zl - r :], y_after[:, :, zl - r :]])
    edge_first = jnp.stack([y_before[:, :, :r], y_after[:, :, :r]])
    corner_before = lax.ppermute(edge_last, "col", z_up)
    corner_after = lax.ppermute(edge_first, "col", z_down)

    def strips(before, after):
        top = jnp.pad(before.transpose(0, 2, 1, 3), ((0, 0), (0, 0), (EDGE - r, 0), (0, 0)))
        low = jnp.pad(after.transpose(0, 2, 1, 3), ((0, 0), (0, 0), (0, EDGE - r), (0, 0)))
        return jnp.stack([top, low])

    y_strips = strips(y_before, y_after)
    inner = 2 * EDGE
    half = EDGE + inner

    def pair(lead_of, ranges):
        return tuple((lead_of(f), ranges) for f in range(2))

    y_edges = dict(
        name="y_edges", rows=2 * half, rows_out=2 * EDGE, length=length, planes=zl,
        slabs=inner_slabs, z_used=(EDGE - r, zl - EDGE + r),
        slab_start=lambda s: EDGE - r + SLAB * s, slab_out=lambda s: EDGE + SLAB * s,
        groups=((EDGE, EDGE, 0), (half + EDGE, EDGE, yl - EDGE)),
        copies=[
            ((2, 2), pair(lambda f: (0, f), ((0, zl), (0, EDGE), (0, length))),
             ((0, zl), (0, EDGE), (0, length))),
            ((0, 1), pair(lambda f: (), ((0, zl), (0, inner), (0, length))),
             ((0, zl), (EDGE, inner), (0, length))),
            ((0, 1), pair(lambda f: (), ((0, zl), (yl - inner, inner), (0, length))),
             ((0, zl), (half, inner), (0, length))),
            ((2, 2), pair(lambda f: (1, f), ((0, zl), (0, EDGE), (0, length))),
             ((0, zl), (half + inner, EDGE), (0, length))),
        ],
    )
    out_pos = np.concatenate([y_rows[:EDGE], y_rows[yl - EDGE :]])
    in_pos = np.concatenate([np.arange(-EDGE, inner), np.arange(yl - inner, yl + EDGE)])
    out = run_part(
        y_edges, shape, [level_set, image, y_strips], doubled(out_pos, in_pos), wx, out
    )

    corner_strips = jnp.stack(
        [strips(corner_before[0], corner_before[1]), strips(corner_after[0], corner_after[1])]
    )
    depth = SLAB + 2 * r
    near = depth - r
    copies = []
    for side, (z_halo, z_dst, local_src, local_dst) in enumerate(
        ((4, 0, 0, r), (5, depth + near, zl - near, depth))
    ):
        copies += [
            ((z_halo, z_halo), pair(lambda f: (f,), ((0, r), (0, yl), (0, length))),
             ((z_dst, r), (EDGE, yl), (0, length))),
            ((0, 1), pair(lambda f: (), ((local_src, near), (0, yl), (0, length))),
             ((local_dst, near), (EDGE, yl), (0, length))),
        ]
        for t, row in ((0, 0), (1, EDGE + yl)):
            copies += [
                ((2, 2), pair(lambda f, t=t: (t, f), ((local_src, near), (0, EDGE), (0, length))),
                 ((local_dst, near), (row, EDGE), (0, length))),
                ((3, 3),
                 pair(lambda f, t=t, side=side: (side, t, f), ((0, r), (0, EDGE), (0, length))),
                 ((z_dst, r), (row, EDGE), (0, length))),
            ]
    z_edges = dict(
        name="z_edges", rows=yl + 2 * EDGE, rows_out=yl, length=length, planes=2 * depth,
        slabs=2, z_used=(0, 2 * depth),
        slab_start=lambda s: depth * s, slab_out=lambda s: (zl - EDGE) * s,
        groups=((EDGE, yl, 0),),
        copies=copies,
    )
    return run_part(
        z_edges, shape,
        [level_set, image, y_strips, corner_strips, z_before, z_after],
        doubled(y_rows, np.arange(-EDGE, yl + EDGE)), wx, out,
    )


def solution(mesh):
    return jax.shard_map(
        body,
        mesh=mesh,
        in_specs=(P("col", "row", None), P("col", "row", None)),
        out_specs=P("col", "row", None),
        check_vma=False,
    )
```

```python
import functools
import math

import jax
import jax.numpy as jnp
import numpy as np
from jax import lax
from jax.experimental import pallas as pl
from jax.experimental.pallas import tpu as pltpu
from jax.sharding import PartitionSpec as P

RADIUS = 6
PAIR = 2
EDGE = 8
TILE = 16
LANES = 128

sigma_cells = 8.0
dt_step = 0.5
nu_diff = 0.1
eps_fit = 0.05

ATAN_COEFS = (
    0.318309854, -0.106098923, 0.0635640505, -0.0446161759,
    0.0315320858, -0.0188971351, 0.00769233704, -0.0014861167,
)
TAP_SCALE = 0.519


def taps():
    d = np.arange(RADIUS + 1, dtype=np.float64)
    exact = np.exp(-d * d / (2.0 * sigma_cells * sigma_cells))
    short = np.asarray((TAP_SCALE * exact).astype(np.float32).astype(jnp.bfloat16))
    short64 = short.astype(np.float64)
    short_sum = short64[0] + 2.0 * short64[1:].sum()
    z_taps = exact / (exact[0] + 2.0 * exact[1:].sum()) / (short_sum * short_sum)
    return [float(v) for v in z_taps], short


def band(out_pos, in_pos, period=None):
    _, short = taps()
    dist = np.abs(out_pos[:, None] - in_pos[None, :])
    if period is not None:
        dist = np.minimum(dist, period - dist)
    table = np.where(dist <= RADIUS, short.astype(np.float32)[np.minimum(dist, RADIUS)], 0.0)
    return jnp.asarray(table.astype(np.float32), jnp.bfloat16)


def heaviside(x):
    far = jnp.abs(x) > 1.0
    t = jnp.where(far, 1.0 / x, x)
    z = t * t
    p = ATAN_COEFS[-1]
    for c in ATAN_COEFS[-2::-1]:
        p = p * z + c
    p = p * t
    base = jnp.where(far, jnp.where(x > 0.0, 1.0, 0.0), 0.5)
    return base + jnp.where(far, -p, p)


def interleave(first, second):
    a, b = len(first), len(second)
    done = 0
    for i, piece in enumerate(first):
        piece()
        want = (i + 1) * b // a
        while done < want:
            second[done]()
            done += 1


def split_bf16(acc):
    hi = acc.astype(jnp.bfloat16)
    return hi, (acc - hi.astype(jnp.float32)).astype(jnp.bfloat16)


def part_kernel(plan, *refs):
    srcs, wys, wx_ref, _, outs, scratch = plan["unpack"](refs)
    out_ref = outs[0]
    lev, img, hea, him, sqr, zb0, zb1, xb, xr, ob, in_sem, out_sem, exp_sem = scratch[:13]
    rows, rows_out, length = plan["rows"], plan["rows_out"], plan["length"]
    groups, steps = plan["groups"], plan["steps"]
    z_taps, _ = taps()
    fields = (him, hea, img, sqr)

    def copy_in(k):
        src, lead, src_ranges, dst, dst_ranges = plan["copies"][k]
        src = srcs[src]
        for i in lead:
            src = src.at[i]
        return pltpu.make_async_copy(
            src.at[tuple(pl.ds(a, n) for a, n in src_ranges)],
            scratch[dst].at[tuple(pl.ds(a, n) for a, n in dst_ranges)],
            in_sem.at[k],
        )

    for k in range(len(plan["copies"])):
        copy_in(k).start()

    def fill(z, carry, spans):
        for a, n, compute in spans:
            if compute:
                hea[z, a : a + n, :] = heaviside(lev[z, a : a + n, :])
            im = img[z, a : a + n, :]
            him[z, a : a + n, :] = hea[z, a : a + n, :] * im
            sqr[z, a : a + n, :] = im * im
        return carry

    for waits, (z0, z1), spans in plan["fills"]:
        for k in waits:
            copy_in(k).wait()
        lax.fori_loop(z0, z1, functools.partial(fill, spans=spans), 0)

    exports = []
    for e, (a, n) in enumerate(plan["h_export"]):
        copy = pltpu.make_async_copy(
            hea.at[pl.ds(a, n)], outs[1].at[pl.ds(a, n)], exp_sem.at[e]
        )
        copy.start()
        exports.append(copy)

    def z_tile(first, zb, at, lane, f):
        def emit():
            vals = [
                fields[f][first + z, pl.ds(at, TILE), pl.ds(lane, LANES)]
                for z in range(PAIR + 2 * RADIUS)
            ]
            for z in range(PAIR):
                acc = vals[z + RADIUS] * z_taps[0]
                for d in range(1, RADIUS + 1):
                    acc = acc + (vals[z + RADIUS - d] + vals[z + RADIUS + d]) * z_taps[d]
                hi, lo = split_bf16(acc)
                cols = pl.ds(f * length + lane, LANES)
                zb[z, pl.ds(at, TILE), cols] = hi
                zb[z, pl.ds(at + rows, TILE), cols] = lo

        return emit

    def z_pieces(first, zb, row_starts):
        return [
            z_tile(first, zb, at, lane, f)
            for at in row_starts
            for lane in range(0, length, LANES)
            for f in range(4)
        ]

    wide = 2 * LANES

    def along_y(t, z, zb, col):
        def emit():
            acc = jnp.dot(
                wys[0][...], zb[z, :, col : col + wide], preferred_element_type=jnp.float32
            )
            if plan["ready"]:
                acc = acc + jnp.dot(
                    wys[1][...], scratch[13][PAIR * t + z, :, col : col + wide],
                    preferred_element_type=jnp.float32,
                )
            hi, lo = split_bf16(acc)
            for part in range(0, wide, LANES):
                f, x = divmod(col + part, length)
                at = (z * 4 + f) * rows_out
                xb[at : at + rows_out, x : x + LANES] = hi[:, part : part + LANES]
                xb[at : at + rows_out, length + x : length + x + LANES] = lo[:, part : part + LANES]

        return emit

    def along_x(z):
        def emit():
            at = z * 4 * rows_out
            xr[at : at + 4 * rows_out, :] = jnp.dot(
                xb[at : at + 4 * rows_out, :], wx_ref[...], preferred_element_type=jnp.float32
            )

        return emit

    def update(t, z, zi, row, at):
        def emit():
            s1, s2, s3, s4 = (
                xr[(z * 4 + f) * rows_out + row : (z * 4 + f) * rows_out + row + 8, :]
                for f in range(4)
            )
            lv, im, before, after, above, below = plan["local"](scratch, zi, at)
            inner = s2 + eps_fit
            outer = (1.0 + eps_fit) - s2
            spread = s4 - s3 * s3 + eps_fit
            left = s1 * outer
            right = (s3 - s1) * inner
            prod = inner * outer
            denom = (prod * prod) * (spread * (math.pi * (1.0 + lv * lv)))
            numer = (left - right) * (2.0 * im * prod - (left + right))
            laplace = (
                (before + after)
                + (above + below)
                + (pltpu.roll(lv, 1, 1) + pltpu.roll(lv, length - 1, 1))
                - 6.0 * lv
            )
            ob[PAIR * t + z, row : row + 8, :] = lv + dt_step * (
                nu_diff * laplace + numer / denom
            )

        return emit

    def yxf_pieces(t, zb):
        zi = plan["base"](t) + RADIUS
        pieces = [
            along_y(t, z, zb, col) for z in range(PAIR) for col in range(0, 4 * length, wide)
        ]
        pieces += [along_x(z) for z in range(PAIR)]
        for z in range(PAIR):
            row = 0
            for start, count, _ in groups:
                pieces += [update(t, z, zi + z, row + i, start + i) for i in range(0, count, 8)]
                row += count
        return pieces

    def out_copies(t):
        row, made = 0, []
        for g, (_, count, y0) in enumerate(groups):
            made.append(
                pltpu.make_async_copy(
                    ob.at[pl.ds(PAIR * t, PAIR), pl.ds(row, count), :],
                    out_ref.at[pl.ds(plan["out_z"](t), PAIR), pl.ds(y0, count), :],
                    out_sem.at[t, g],
                )
            )
            row += count
        return made

    n_h = len(plan["h_export"])

    def z_export(t, zb, slot):
        return [
            pltpu.make_async_copy(
                zb.at[:, pl.ds(src, TILE), :],
                outs[2].at[pl.ds(PAIR * t, PAIR), pl.ds(TILE * e, TILE), :],
                exp_sem.at[n_h + len(plan["z_export"]) * slot + e],
            )
            for e, src in enumerate(plan["z_export"])
        ]

    def prologue(r, carry):
        at = pl.multiple_of(r * TILE, TILE)
        for piece in z_pieces(plan["base"](0), zb0, [at]):
            piece()
        return carry

    lax.fori_loop(0, rows // TILE, prologue, 0)
    for copy in z_export(0, zb0, 0):
        copy.start()
    for k in plan["late_waits"]:
        copy_in(k).wait()
    tiles = list(range(0, rows, TILE))

    def two_steps(i, carry):
        for half, (now, nxt) in enumerate(((zb0, zb1), (zb1, zb0))):
            t = 2 * i + half
            after = jnp.minimum(t + 1, steps - 1)
            if not plan["z_export"]:
                pass
            elif half == 0:
                @pl.when(i > 0)
                def _():
                    for copy in z_export(t - 1, nxt, 1):
                        copy.wait()
            else:
                for copy in z_export(t - 1, nxt, 0):
                    copy.wait()
            interleave(yxf_pieces(t, now), z_pieces(plan["base"](after), nxt, tiles))
            for copy in out_copies(t):
                copy.start()
            if not plan["z_export"]:
                pass
            elif half == 0:
                for copy in z_export(t + 1, nxt, 1):
                    copy.start()
            else:
                @pl.when(i + 1 < steps // 2)
                def _():
                    for copy in z_export(t + 1, nxt, 0):
                        copy.start()
        return carry

    lax.fori_loop(0, steps // 2, two_steps, 0)
    for copy in z_export(steps - 1, zb1, 1):
        copy.wait()
    for copy in exports:
        copy.wait()

    def finish(t, carry):
        for copy in out_copies(t):
            copy.wait()
        return carry

    lax.fori_loop(0, steps, finish, 0)


def run_part(plan, shape, srcs, wys, wx, prev):
    rows, rows_out, length, planes = plan["rows"], plan["rows_out"], plan["length"], plan["planes"]
    steps, n_ready = plan["steps"], plan.get("ready", 0)
    n_src, n_wy, n_out = len(srcs), len(wys), 1 + len(plan["extra_out"])
    n_prev = 0 if prev is None else 1

    def unpack(refs):
        cuts = np.cumsum([n_src, n_wy, 1, n_prev, n_out])
        a, b, c, d, e = (int(v) for v in cuts)
        return refs[:a], refs[a:b], refs[b], refs[c:d], refs[d:e], refs[e:]

    plan = dict(plan, unpack=unpack, ready=n_ready)
    any_spec = pl.BlockSpec(memory_space=pl.ANY)
    vmem = pl.BlockSpec(memory_space=pltpu.VMEM)
    args = list(srcs) + list(wys) + [wx] + ([] if prev is None else [prev])
    specs = [any_spec] * n_src + [vmem] * (n_wy + 1) + [any_spec] * n_prev
    n_elem = PAIR * steps * rows_out * length
    field = pltpu.VMEM((planes, rows, length), jnp.float32)
    taps_buffer = pltpu.VMEM((PAIR, 2 * rows, 4 * length), jnp.bfloat16)
    scratch = [field] * 5 + [
        taps_buffer,
        taps_buffer,
        pltpu.VMEM((PAIR * 4 * rows_out, 2 * length), jnp.bfloat16),
        pltpu.VMEM((PAIR * 4 * rows_out, length), jnp.float32),
        pltpu.VMEM((PAIR * steps, rows_out, length), jnp.float32),
        pltpu.SemaphoreType.DMA((len(plan["copies"]),)),
        pltpu.SemaphoreType.DMA((steps, len(plan["groups"]))),
        pltpu.SemaphoreType.DMA((max(1, len(plan["h_export"]) + 2 * len(plan["z_export"])),)),
    ]
    if n_ready:
        scratch += [
            pltpu.VMEM((PAIR * steps, n_ready, 4 * length), jnp.bfloat16),
            pltpu.VMEM((planes, 2 * (EDGE + TILE), length), jnp.float32),
            pltpu.VMEM((planes, 2 * (EDGE + TILE), length), jnp.float32),
        ]
    out = pl.pallas_call(
        functools.partial(part_kernel, plan),
        out_shape=[jax.ShapeDtypeStruct(shape, jnp.float32)] + plan["extra_out"],
        in_specs=specs,
        out_specs=[any_spec] * n_out,
        scratch_shapes=scratch,
        input_output_aliases={} if prev is None else {len(args) - 1: 0},
        compiler_params=pltpu.CompilerParams(vmem_limit_bytes=60 * 1024 * 1024),
        cost_estimate=pl.CostEstimate(
            flops=n_elem * 12000, bytes_accessed=n_elem * 12, transcendentals=0
        ),
        name=plan["name"],
    )(*args)
    return out


def neighbours(axis):
    n = lax.axis_size(axis)
    up = [(i, (i + 1) % n) for i in range(n)]
    return up, [(j, i) for i, j in up]


def local_of(lev_at, img_at):
    def local(scratch, zi, at):
        lev, img = scratch[lev_at], scratch[img_at]
        return (
            lev[zi, at : at + 8, :],
            img[zi, at : at + 8, :],
            lev[zi - 1, at : at + 8, :],
            lev[zi + 1, at : at + 8, :],
            lev[zi, at - 1 : at + 7, :],
            lev[zi, at + 1 : at + 9, :],
        )

    return local


LEV, IMG, HEA, READY, NEAR_LEV, NEAR_IMG = 0, 1, 2, 13, 14, 15


def body(level_set, image):
    zl, yl, length = level_set.shape
    shape = level_set.shape
    r = RADIUS
    both = jnp.stack([level_set, image])
    y_up, y_down = neighbours("row")
    z_up, z_down = neighbours("col")

    y_before = lax.ppermute(both[:, :, yl - r :, :].transpose(0, 2, 1, 3), "row", y_up)
    y_after = lax.ppermute(both[:, :, :r, :].transpose(0, 2, 1, 3), "row", y_down)
    z_before = lax.ppermute(both[:, zl - r :], "col", z_up)
    z_after = lax.ppermute(both[:, :r], "col", z_down)

    y_rows = np.arange(yl)
    wx1 = band(np.arange(length), np.arange(length), length)
    wx = jnp.concatenate([wx1, wx1], axis=0)

    def doubled(out_pos, in_pos):
        w = band(out_pos, in_pos)
        return jnp.concatenate([w, w], axis=1)

    def full(z0, zn, y0, yn):
        return ((z0, zn), (y0, yn), (0, length))

    depth = PAIR * 4 + 2 * r
    near = depth - r
    inner_steps = (zl - 2 * EDGE) // PAIR
    chunk = zl // 3
    interior = dict(
        name="interior", rows=yl, rows_out=yl - 2 * EDGE, length=length, planes=zl,
        steps=inner_steps,
        base=lambda t: EDGE - r + PAIR * t, out_z=lambda t: EDGE + PAIR * t,
        groups=((EDGE, yl - 2 * EDGE, EDGE),), local=local_of(LEV, IMG),
        copies=[
            (f, (), full(z, chunk, 0, yl), f, full(z, chunk, 0, yl))
            for z in range(0, zl, chunk) for f in (LEV, IMG)
        ],
        fills=[
            ((2 * c, 2 * c + 1), (c * chunk, (c + 1) * chunk), ((0, yl, True),)) for c in range(3)
        ],
        h_export=((0, near), (zl - near, near)),
        z_export=(0, yl - TILE, yl, 2 * yl - TILE),
        late_waits=(),
        extra_out=[
            jax.ShapeDtypeStruct(shape, jnp.float32),
            jax.ShapeDtypeStruct((PAIR * inner_steps, 4 * TILE, 4 * length), jnp.bfloat16),
        ],
    )
    out, hea, near_rows = run_part(
        interior, shape, [level_set, image],
        [doubled(y_rows[EDGE : yl - EDGE], y_rows)], wx, None,
    )

    edge_last = jnp.stack([y_before[:, :, zl - r :], y_after[:, :, zl - r :]])
    edge_first = jnp.stack([y_before[:, :, :r], y_after[:, :, :r]])
    corner_before = lax.ppermute(edge_last, "col", z_up)
    corner_after = lax.ppermute(edge_first, "col", z_down)

    def strips(before, after):
        top = jnp.pad(before.transpose(0, 2, 1, 3), ((0, 0), (0, 0), (EDGE - r, 0), (0, 0)))
        low = jnp.pad(after.transpose(0, 2, 1, 3), ((0, 0), (0, 0), (0, EDGE - r), (0, 0)))
        return jnp.stack([top, low])

    y_strips = strips(y_before, y_after)
    half = EDGE + TILE
    z_lo, z_n = EDGE - r, zl - 2 * (EDGE - r)
    copies = [
        (2, (side, f), full(z_lo, z_n, 0, EDGE), f, full(z_lo, z_n, side * EDGE, EDGE))
        for side in range(2) for f in (LEV, IMG)
    ]
    n_first = len(copies)
    for f, dst in ((0, NEAR_LEV), (1, NEAR_IMG)):
        copies += [
            (2, (0, f), full(z_lo, z_n, 0, EDGE), dst, full(z_lo, z_n, 0, EDGE)),
            (f, (), full(z_lo, z_n, 0, TILE), dst, full(z_lo, z_n, EDGE, TILE)),
            (f, (), full(z_lo, z_n, yl - TILE, TILE), dst, full(z_lo, z_n, half, TILE)),
            (2, (1, f), full(z_lo, z_n, 0, EDGE), dst, full(z_lo, z_n, half + TILE, EDGE)),
        ]
    ready_all = ((0, PAIR * inner_steps), (0, 4 * TILE), (0, 4 * length))
    copies.append((3, (), ready_all, READY, ready_all))
    y_edges = dict(
        name="y_edges", rows=2 * EDGE, rows_out=2 * EDGE, length=length, planes=zl,
        steps=inner_steps,
        base=lambda t: EDGE - r + PAIR * t, out_z=lambda t: EDGE + PAIR * t,
        groups=((EDGE, EDGE, 0), (half + EDGE, EDGE, yl - EDGE)),
        local=local_of(NEAR_LEV, NEAR_IMG),
        copies=copies,
        fills=[(tuple(range(n_first)), (z_lo, z_lo + z_n), ((0, 2 * EDGE, True),))],
        h_export=(), z_export=(), late_waits=tuple(range(n_first, len(copies))),
        extra_out=[], ready=4 * TILE,
    )
    out_pos = np.concatenate([y_rows[:EDGE], y_rows[yl - EDGE :]])
    halo_pos = np.concatenate([np.arange(-EDGE, 0), np.arange(yl, yl + EDGE)])
    near_pos = np.concatenate([np.arange(TILE), np.arange(yl - TILE, yl)])
    (out,) = run_part(
        y_edges, shape, [level_set, image, y_strips, near_rows],
        [doubled(out_pos, halo_pos), doubled(out_pos, near_pos)], wx, out,
    )

    corner_strips = jnp.stack(
        [strips(corner_before[0], corner_before[1]), strips(corner_after[0], corner_after[1])]
    )
    rows = yl + 2 * EDGE
    halo_copies, near_copies = [], []
    for side, (z_dst, src, dst) in enumerate(
        ((0, 0, r), (depth + near, zl - near, depth))
    ):
        near_copies.append((6, (), full(src, near, 0, yl), HEA, full(dst, near, EDGE, yl)))
        for f in (LEV, IMG):
            halo_copies.append(
                (4 + side, (f,), full(0, r, 0, yl), f, full(z_dst, r, EDGE, yl))
            )
            near_copies.append((f, (), full(src, near, 0, yl), f, full(dst, near, EDGE, yl)))
            for t, row in ((0, 0), (1, EDGE + yl)):
                halo_copies.append(
                    (3, (side, t, f), full(0, r, 0, EDGE), f, full(z_dst, r, row, EDGE))
                )
                near_copies.append(
                    (2, (t, f), full(src, near, 0, EDGE), f, full(dst, near, row, EDGE))
                )
    copies = halo_copies + near_copies
    whole = ((0, rows, True),)
    z_edges = dict(
        name="z_edges", rows=rows, rows_out=yl, length=length, planes=2 * depth, steps=8,
        base=lambda t: depth * (t // 4) + PAIR * (t % 4),
        out_z=lambda t: (zl - EDGE) * (t // 4) + PAIR * (t % 4),
        groups=((EDGE, yl, 0),), local=local_of(LEV, IMG),
        copies=copies,
        fills=[
            (tuple(range(len(halo_copies))), (0, r), whole),
            ((), (depth + near, 2 * depth), whole),
            (
                tuple(range(len(halo_copies), len(copies))), (r, depth + near),
                ((0, EDGE, True), (EDGE, yl, False), (EDGE + yl, EDGE, True)),
            ),
        ],
        h_export=(), z_export=(), late_waits=(), extra_out=[],
    )
    (out,) = run_part(
        z_edges, shape,
        [level_set, image, y_strips, corner_strips, z_before, z_after, hea],
        [doubled(y_rows, np.arange(-EDGE, yl + EDGE))], wx, out,
    )
    return out


def solution(mesh):
    return jax.shard_map(
        body,
        mesh=mesh,
        in_specs=(P("col", "row", None), P("col", "row", None)),
        out_specs=P("col", "row", None),
        check_vma=False,
    )
```

```python
import functools
import math

import jax
import jax.numpy as jnp
import numpy as np
from jax import lax
from jax.experimental import pallas as pl
from jax.experimental.pallas import tpu as pltpu
from jax.sharding import PartitionSpec as P

RADIUS = 6
PAIR = 2
EDGE = 8
TILE = 16
LANES = 128

sigma_cells = 8.0
dt_step = 0.5
nu_diff = 0.1
eps_fit = 0.05

ATAN_COEFS = (
    0.318309854, -0.106098923, 0.0635640505, -0.0446161759,
    0.0315320858, -0.0188971351, 0.00769233704, -0.0014861167,
)
TAP_SCALE = 0.519


def taps():
    d = np.arange(RADIUS + 1, dtype=np.float64)
    exact = np.exp(-d * d / (2.0 * sigma_cells * sigma_cells))
    short = np.asarray((TAP_SCALE * exact).astype(np.float32).astype(jnp.bfloat16))
    short64 = short.astype(np.float64)
    short_sum = short64[0] + 2.0 * short64[1:].sum()
    z_taps = exact / (exact[0] + 2.0 * exact[1:].sum()) / (short_sum * short_sum)
    return [float(v) for v in z_taps], short


def band(out_pos, in_pos, period=None):
    _, short = taps()
    dist = np.abs(out_pos[:, None] - in_pos[None, :])
    if period is not None:
        dist = np.minimum(dist, period - dist)
    table = np.where(dist <= RADIUS, short.astype(np.float32)[np.minimum(dist, RADIUS)], 0.0)
    return jnp.asarray(table.astype(np.float32), jnp.bfloat16)


def heaviside(x):
    far = jnp.abs(x) > 1.0
    t = jnp.where(far, pl.reciprocal(x, approx=False), x)
    z = t * t
    p = ATAN_COEFS[-1]
    for c in ATAN_COEFS[-2::-1]:
        p = p * z + c
    p = p * t
    base = jnp.where(far, jnp.where(x > 0.0, 1.0, 0.0), 0.5)
    return base + jnp.where(far, -p, p)


def interleave(first, second):
    a, b = len(first), len(second)
    done = 0
    for i, piece in enumerate(first):
        piece()
        want = (i + 1) * b // a
        while done < want:
            second[done]()
            done += 1


def split_bf16(acc):
    hi = acc.astype(jnp.bfloat16)
    return hi, (acc - hi.astype(jnp.float32)).astype(jnp.bfloat16)


def part_kernel(plan, *refs):
    srcs, wys, wx_ref, _, outs, scratch = plan["unpack"](refs)
    out_ref = outs[0]
    lev, img, hea, him, sqr, zb0, zb1, xb, xr, ob, in_sem, out_sem, exp_sem = scratch[:13]
    rows, rows_out, length = plan["rows"], plan["rows_out"], plan["length"]
    groups, steps = plan["groups"], plan["steps"]
    z_taps, _ = taps()
    fields = (him, hea, img, sqr)

    def copy_in(k):
        src, lead, src_ranges, dst, dst_lead, dst_ranges = plan["copies"][k]
        src, dst = srcs[src], scratch[dst]
        for i in lead:
            src = src.at[i]
        for i in dst_lead:
            dst = dst.at[i]
        return pltpu.make_async_copy(
            src.at[tuple(pl.ds(a, n) for a, n in src_ranges)],
            dst.at[tuple(pl.ds(a, n) for a, n in dst_ranges)],
            in_sem.at[k],
        )

    for k in range(len(plan["copies"])):
        copy_in(k).start()

    def transpose_strips():
        held, strip = scratch[16], scratch[17]
        for k in plan["strip_waits"]:
            copy_in(k).wait()
        n_z = held.shape[3]

        def block(b, carry):
            z0 = pl.multiple_of(b * 8, 8)
            for side in range(2):
                for f in range(2):
                    for row in range(EDGE):
                        y = max(row - (EDGE - RADIUS), 0) if side == 0 else min(row, RADIUS - 1)
                        for lane in range(0, length, LANES):
                            strip[
                                side, f, lane // LANES, pl.ds(z0 * EDGE + row, 8, stride=EDGE), :
                            ] = held[side, f, y, pl.ds(z0, 8), pl.ds(lane, LANES)]
            return carry

        lax.fori_loop(0, n_z // 8, block, 0)
        copy = pltpu.make_async_copy(strip, outs[1], exp_sem.at[0])
        copy.start()

        def spread(z, carry):
            rows8 = pl.ds(pl.multiple_of(z * EDGE, EDGE), EDGE)
            for side in range(2):
                for f, (halo, near) in enumerate(((lev, scratch[14]), (img, scratch[15]))):
                    at = side * (near.shape[1] - EDGE)
                    for lane in range(0, length, LANES):
                        v = strip[side, f, lane // LANES, rows8, :]
                        halo[z, side * EDGE : (side + 1) * EDGE, lane : lane + LANES] = v
                        near[z, at : at + EDGE, lane : lane + LANES] = v
            return carry

        lax.fori_loop(0, n_z, spread, 0)
        return copy

    strip_copy = transpose_strips() if plan["strip_waits"] else None

    def fill(z, carry, spans):
        for a, n, compute in spans:
            for at in range(a, a + n, 8):
                for lane in range(0, length, LANES):
                    where = (z, pl.ds(at, 8), pl.ds(lane, LANES))
                    if compute:
                        h = heaviside(lev[where])
                        hea[where] = h
                    else:
                        h = hea[where]
                    im = img[where]
                    him[where] = h * im
                    sqr[where] = im * im
        return carry

    for waits, (z0, z1), spans in plan["fills"]:
        for k in waits:
            copy_in(k).wait()
        lax.fori_loop(z0, z1, functools.partial(fill, spans=spans), 0)

    exports = []
    for e, (a, n) in enumerate(plan["h_export"]):
        copy = pltpu.make_async_copy(
            hea.at[pl.ds(a, n)], outs[1].at[pl.ds(a, n)], exp_sem.at[e]
        )
        copy.start()
        exports.append(copy)

    def z_tile(first, zb, at, lane, f):
        def emit():
            vals = [
                fields[f][first + z, pl.ds(at, TILE), pl.ds(lane, LANES)]
                for z in range(PAIR + 2 * RADIUS)
            ]
            for z in range(PAIR):
                acc = vals[z + RADIUS] * z_taps[0]
                for d in range(1, RADIUS + 1):
                    acc = acc + (vals[z + RADIUS - d] + vals[z + RADIUS + d]) * z_taps[d]
                hi, lo = split_bf16(acc)
                cols = pl.ds(f * length + lane, LANES)
                zb[z, pl.ds(at, TILE), cols] = hi
                zb[z, pl.ds(at + rows, TILE), cols] = lo

        return emit

    def z_pieces(first, zb, row_starts):
        return [
            z_tile(first, zb, at, lane, f)
            for at in row_starts
            for lane in range(0, length, LANES)
            for f in range(4)
        ]

    wide = 2 * LANES

    def along_y(t, z, zb, col):
        def emit():
            acc = jnp.dot(
                wys[0][...], zb[z, :, col : col + wide], preferred_element_type=jnp.float32
            )
            if plan["ready"]:
                acc = acc + jnp.dot(
                    wys[1][...], scratch[13][PAIR * t + z, :, col : col + wide],
                    preferred_element_type=jnp.float32,
                )
            hi, lo = split_bf16(acc)
            for part in range(0, wide, LANES):
                f, x = divmod(col + part, length)
                at = (z * 4 + f) * rows_out
                xb[at : at + rows_out, x : x + LANES] = hi[:, part : part + LANES]
                xb[at : at + rows_out, length + x : length + x + LANES] = lo[:, part : part + LANES]

        return emit

    def along_x(z, planes):
        def emit():
            at, n = z * 4 * rows_out, planes * 4 * rows_out
            xr[at : at + n, :] = jnp.dot(
                xb[at : at + n, :], wx_ref[...], preferred_element_type=jnp.float32
            )

        return emit

    def update(t, z, zi, row, at):
        def emit():
            for lane in range(0, length, LANES):
                s1, s2, s3, s4 = (
                    xr[
                        (z * 4 + f) * rows_out + row : (z * 4 + f) * rows_out + row + 8,
                        lane : lane + LANES,
                    ]
                    for f in range(4)
                )
                lv, im, others = plan["local"](scratch, zi, at, lane, length)
                inner = s2 + eps_fit
                outer = (1.0 + eps_fit) - s2
                spread = s4 - (s3 * s3 - eps_fit)
                left = s1 * outer
                right = (s3 - s1) * inner
                prod = inner * outer
                pi_dt = math.pi / dt_step
                denom = (prod * prod) * (spread * (pi_dt + (pi_dt * lv) * lv))
                numer = (left - right) * ((im + im) * prod - (left + right))
                ob[PAIR * t + z, row : row + 8, lane : lane + LANES] = (
                    (1.0 - 6.0 * dt_step * nu_diff) * lv
                    + (dt_step * nu_diff) * others
                    + numer * pl.reciprocal(denom, approx=False)
                )

        return emit

    def yxf_pieces(t, zb):
        zi = plan["base"](t) + RADIUS
        pieces = [
            along_y(t, z, zb, col) for z in range(PAIR) for col in range(0, 4 * length, wide)
        ]
        together = PAIR if PAIR * rows_out <= 64 else 1
        pieces += [along_x(z, together) for z in range(0, PAIR, together)]
        for z in range(PAIR):
            row = 0
            for start, count, _ in groups:
                pieces += [update(t, z, zi + z, row + i, start + i) for i in range(0, count, 8)]
                row += count
        return pieces

    def out_copies(t):
        row, made = 0, []
        for g, (_, count, y0) in enumerate(groups):
            made.append(
                pltpu.make_async_copy(
                    ob.at[pl.ds(PAIR * t, PAIR), pl.ds(row, count), :],
                    out_ref.at[pl.ds(plan["out_z"](t), PAIR), pl.ds(y0, count), :],
                    out_sem.at[t, g],
                )
            )
            row += count
        return made

    n_h = len(plan["h_export"])

    def z_export(t, zb, slot):
        return [
            pltpu.make_async_copy(
                zb.at[:, pl.ds(src, TILE), :],
                outs[2].at[pl.ds(PAIR * t, PAIR), pl.ds(TILE * e, TILE), :],
                exp_sem.at[n_h + len(plan["z_export"]) * slot + e],
            )
            for e, src in enumerate(plan["z_export"])
        ]

    def prologue(r, carry):
        at = pl.multiple_of(r * TILE, TILE)
        for piece in z_pieces(plan["base"](0), zb0, [at]):
            piece()
        return carry

    lax.fori_loop(0, rows // TILE, prologue, 0)
    for copy in z_export(0, zb0, 0):
        copy.start()
    for k in plan["late_waits"]:
        copy_in(k).wait()
    tiles = list(range(0, rows, TILE))

    def two_steps(i, carry):
        for half, (now, nxt) in enumerate(((zb0, zb1), (zb1, zb0))):
            t = 2 * i + half
            after = jnp.minimum(t + 1, steps - 1)
            if not plan["z_export"]:
                pass
            elif half == 0:
                @pl.when(i > 0)
                def _():
                    for copy in z_export(t - 1, nxt, 1):
                        copy.wait()
            else:
                for copy in z_export(t - 1, nxt, 0):
                    copy.wait()
            interleave(yxf_pieces(t, now), z_pieces(plan["base"](after), nxt, tiles))
            for copy in out_copies(t):
                copy.start()
            if not plan["z_export"]:
                pass
            elif half == 0:
                for copy in z_export(t + 1, nxt, 1):
                    copy.start()
            else:
                @pl.when(i + 1 < steps // 2)
                def _():
                    for copy in z_export(t + 1, nxt, 0):
                        copy.start()
        return carry

    lax.fori_loop(0, steps // 2, two_steps, 0)
    for copy in z_export(steps - 1, zb1, 1):
        copy.wait()
    for copy in exports + ([] if strip_copy is None else [strip_copy]):
        copy.wait()

    def finish(t, carry):
        for copy in out_copies(t):
            copy.wait()
        return carry

    lax.fori_loop(0, steps, finish, 0)


def run_part(plan, shape, srcs, wys, wx, prev):
    rows, rows_out, length, planes = plan["rows"], plan["rows_out"], plan["length"], plan["planes"]
    steps, n_ready = plan["steps"], plan.get("ready", 0)
    n_src, n_wy, n_out = len(srcs), len(wys), 1 + len(plan["extra_out"])
    n_prev = 0 if prev is None else 1

    def unpack(refs):
        cuts = np.cumsum([n_src, n_wy, 1, n_prev, n_out])
        a, b, c, d, e = (int(v) for v in cuts)
        return refs[:a], refs[a:b], refs[b], refs[c:d], refs[d:e], refs[e:]

    plan = dict(plan, unpack=unpack, ready=n_ready, strip_waits=plan.get("strip_waits", ()))
    any_spec = pl.BlockSpec(memory_space=pl.ANY)
    vmem = pl.BlockSpec(memory_space=pltpu.VMEM)
    args = list(srcs) + list(wys) + [wx] + ([] if prev is None else [prev])
    specs = [any_spec] * n_src + [vmem] * (n_wy + 1) + [any_spec] * n_prev
    n_elem = PAIR * steps * rows_out * length
    field = pltpu.VMEM((planes, rows, length), jnp.float32)
    taps_buffer = pltpu.VMEM((PAIR, 2 * rows, 4 * length), jnp.bfloat16)
    scratch = [field] * 5 + [
        taps_buffer,
        taps_buffer,
        pltpu.VMEM((PAIR * 4 * rows_out, 2 * length), jnp.bfloat16),
        pltpu.VMEM((PAIR * 4 * rows_out, length), jnp.float32),
        pltpu.VMEM((PAIR * steps, rows_out, length), jnp.float32),
        pltpu.SemaphoreType.DMA((len(plan["copies"]),)),
        pltpu.SemaphoreType.DMA((steps, len(plan["groups"]))),
        pltpu.SemaphoreType.DMA((max(1, len(plan["h_export"]) + 2 * len(plan["z_export"])),)),
    ]
    if n_ready:
        scratch += [
            pltpu.VMEM((PAIR * steps, n_ready, 4 * length), jnp.bfloat16),
            pltpu.VMEM((planes, 2 * (EDGE + TILE), length), jnp.float32),
            pltpu.VMEM((planes, 2 * (EDGE + TILE), length), jnp.float32),
            pltpu.VMEM((2, 2, RADIUS, planes, length), jnp.float32),
            pltpu.VMEM((2, 2, length // LANES, planes * EDGE, LANES), jnp.float32),
        ]
    out = pl.pallas_call(
        functools.partial(part_kernel, plan),
        out_shape=[jax.ShapeDtypeStruct(shape, jnp.float32)] + plan["extra_out"],
        in_specs=specs,
        out_specs=[any_spec] * n_out,
        scratch_shapes=scratch,
        input_output_aliases={} if prev is None else {len(args) - 1: 0},
        compiler_params=pltpu.CompilerParams(
            vmem_limit_bytes=60 * 1024 * 1024,
        ),
        cost_estimate=pl.CostEstimate(
            flops=n_elem * 12000, bytes_accessed=n_elem * 12, transcendentals=0
        ),
        name=plan["name"],
    )(*args)
    return out


def neighbours(axis):
    n = lax.axis_size(axis)
    up = [(i, (i + 1) % n) for i in range(n)]
    return up, [(j, i) for i, j in up]


def local_of(lev_at, img_at):
    def local(scratch, zi, at, lane, length):
        lev, img = scratch[lev_at], scratch[img_at]
        cols = slice(lane, lane + LANES)
        lv = lev[zi, at : at + 8, cols]
        last = LANES - 1
        prev = lev[zi, at : at + 8, (lane - LANES) % length : (lane - LANES) % length + LANES]
        follow = lev[zi, at : at + 8, (lane + LANES) % length : (lane + LANES) % length + LANES]
        index = lax.broadcasted_iota(jnp.int32, (8, LANES), 1)
        here_up, here_down = pltpu.roll(lv, 1, 1), pltpu.roll(lv, last, 1)
        west = jnp.where(index == 0, pltpu.roll(prev, 1, 1), here_up)
        east = jnp.where(index == last, pltpu.roll(follow, last, 1), here_down)
        others = (
            (lev[zi - 1, at : at + 8, cols] + lev[zi + 1, at : at + 8, cols])
            + (lev[zi, at - 1 : at + 7, cols] + lev[zi, at + 1 : at + 9, cols])
            + (west + east)
        )
        return lv, img[zi, at : at + 8, cols], others

    return local


LEV, IMG, HEA, READY, NEAR_LEV, NEAR_IMG, HELD = 0, 1, 2, 13, 14, 15, 16


def body(level_set, image):
    zl, yl, length = level_set.shape
    shape = level_set.shape
    r = RADIUS
    both = jnp.stack([level_set, image])
    y_up, y_down = neighbours("row")
    z_up, z_down = neighbours("col")

    y_before = lax.ppermute(both[:, :, yl - r :, :].transpose(0, 2, 1, 3), "row", y_up)
    y_after = lax.ppermute(both[:, :, :r, :].transpose(0, 2, 1, 3), "row", y_down)
    z_before = lax.ppermute(both[:, zl - r :], "col", z_up)
    z_after = lax.ppermute(both[:, :r], "col", z_down)

    y_rows = np.arange(yl)
    wx1 = band(np.arange(length), np.arange(length), length)
    wx = jnp.concatenate([wx1, wx1], axis=0)

    def doubled(out_pos, in_pos):
        w = band(out_pos, in_pos)
        return jnp.concatenate([w, w], axis=1)

    def full(z0, zn, y0, yn):
        return ((z0, zn), (y0, yn), (0, length))

    depth = PAIR * 4 + 2 * r
    near = depth - r
    inner_steps = (zl - 2 * EDGE) // PAIR
    chunk = zl // 3
    interior = dict(
        name="interior", rows=yl, rows_out=yl - 2 * EDGE, length=length, planes=zl,
        steps=inner_steps,
        base=lambda t: EDGE - r + PAIR * t, out_z=lambda t: EDGE + PAIR * t,
        groups=((EDGE, yl - 2 * EDGE, EDGE),), local=local_of(LEV, IMG),
        copies=[
            (f, (), full(z, chunk, 0, yl), f, (), full(z, chunk, 0, yl))
            for z in range(0, zl, chunk) for f in (LEV, IMG)
        ],
        fills=[
            ((2 * c, 2 * c + 1), (c * chunk, (c + 1) * chunk), ((0, yl, True),)) for c in range(3)
        ],
        h_export=((0, near), (zl - near, near)),
        z_export=(0, yl - TILE, yl, 2 * yl - TILE),
        late_waits=(),
        extra_out=[
            jax.ShapeDtypeStruct(shape, jnp.float32),
            jax.ShapeDtypeStruct((PAIR * inner_steps, 4 * TILE, 4 * length), jnp.bfloat16),
        ],
    )
    out, hea, near_rows = run_part(
        interior, shape, [level_set, image],
        [doubled(y_rows[EDGE : yl - EDGE], y_rows)], wx, None,
    )

    edge_last = jnp.stack([y_before[:, :, zl - r :], y_after[:, :, zl - r :]])
    edge_first = jnp.stack([y_before[:, :, :r], y_after[:, :, :r]])
    corner_before = lax.ppermute(edge_last, "col", z_up)
    corner_after = lax.ppermute(edge_first, "col", z_down)

    def strips(before, after):
        top = jnp.pad(before.transpose(0, 2, 1, 3), ((0, 0), (0, 0), (EDGE - r, 0), (0, 0)))
        low = jnp.pad(after.transpose(0, 2, 1, 3), ((0, 0), (0, 0), (0, EDGE - r), (0, 0)))
        return jnp.stack([top, low])

    half = EDGE + TILE
    z_lo, z_n = EDGE - r, zl - 2 * (EDGE - r)
    halo = ((0, r), (0, zl), (0, length))
    copies = [(2 + side, (f,), halo, HELD, (side, f), halo) for side in range(2) for f in range(2)]
    n_first = len(copies)
    for f, dst in ((0, NEAR_LEV), (1, NEAR_IMG)):
        copies += [
            (f, (), full(z_lo, z_n, 0, TILE), dst, (), full(z_lo, z_n, EDGE, TILE)),
            (f, (), full(z_lo, z_n, yl - TILE, TILE), dst, (), full(z_lo, z_n, half, TILE)),
        ]
    ready_all = ((0, PAIR * inner_steps), (0, 4 * TILE), (0, 4 * length))
    copies.append((4, (), ready_all, READY, (), ready_all))
    y_edges = dict(
        name="y_edges", rows=2 * EDGE, rows_out=2 * EDGE, length=length, planes=zl,
        steps=inner_steps,
        base=lambda t: EDGE - r + PAIR * t, out_z=lambda t: EDGE + PAIR * t,
        groups=((EDGE, EDGE, 0), (half + EDGE, EDGE, yl - EDGE)),
        local=local_of(NEAR_LEV, NEAR_IMG),
        copies=copies,
        fills=[((), (z_lo, z_lo + z_n), ((0, 2 * EDGE, True),))],
        h_export=(), z_export=(), late_waits=tuple(range(n_first, len(copies))),
        extra_out=[
            jax.ShapeDtypeStruct((2, 2, length // LANES, zl * EDGE, LANES), jnp.float32)
        ],
        ready=4 * TILE, strip_waits=tuple(range(n_first)),
    )
    out_pos = np.concatenate([y_rows[:EDGE], y_rows[yl - EDGE :]])
    halo_pos = np.concatenate([np.arange(-EDGE, 0), np.arange(yl, yl + EDGE)])
    near_pos = np.concatenate([np.arange(TILE), np.arange(yl - TILE, yl)])
    out, y_strips = run_part(
        y_edges, shape, [level_set, image, y_before, y_after, near_rows],
        [doubled(out_pos, halo_pos), doubled(out_pos, near_pos)], wx, out,
    )
    y_strips = y_strips.reshape(2, 2, length // LANES, zl, EDGE, LANES)

    corner_strips = jnp.stack(
        [strips(corner_before[0], corner_before[1]), strips(corner_after[0], corner_after[1])]
    )
    rows = yl + 2 * EDGE
    halo_copies, near_copies = [], []
    for side, (z_dst, src, dst) in enumerate(
        ((0, 0, r), (depth + near, zl - near, depth))
    ):
        near_copies.append((6, (), full(src, near, 0, yl), HEA, (), full(dst, near, EDGE, yl)))
        for f in (LEV, IMG):
            halo_copies.append(
                (4 + side, (f,), full(0, r, 0, yl), f, (), full(z_dst, r, EDGE, yl))
            )
            near_copies.append((f, (), full(src, near, 0, yl), f, (), full(dst, near, EDGE, yl)))
            for t, row in ((0, 0), (1, EDGE + yl)):
                halo_copies.append(
                    (3, (side, t, f), full(0, r, 0, EDGE), f, (), full(z_dst, r, row, EDGE))
                )
                near_copies += [
                    (
                        2, (t, f, lane // LANES), ((src, near), (0, EDGE), (0, LANES)),
                        f, (), ((dst, near), (row, EDGE), (lane, LANES)),
                    )
                    for lane in range(0, length, LANES)
                ]
    copies = halo_copies + near_copies
    whole = ((0, rows, True),)
    z_edges = dict(
        name="z_edges", rows=rows, rows_out=yl, length=length, planes=2 * depth, steps=8,
        base=lambda t: depth * (t // 4) + PAIR * (t % 4),
        out_z=lambda t: (zl - EDGE) * (t // 4) + PAIR * (t % 4),
        groups=((EDGE, yl, 0),), local=local_of(LEV, IMG),
        copies=copies,
        fills=[
            (tuple(range(len(halo_copies))), (0, r), whole),
            ((), (depth + near, 2 * depth), whole),
            (
                tuple(range(len(halo_copies), len(copies))), (r, depth + near),
                ((0, EDGE, True), (EDGE, yl, False), (EDGE + yl, EDGE, True)),
            ),
        ],
        h_export=(), z_export=(), late_waits=(), extra_out=[],
    )
    (out,) = run_part(
        z_edges, shape,
        [level_set, image, y_strips, corner_strips, z_before, z_after, hea],
        [doubled(y_rows, np.arange(-EDGE, yl + EDGE))], wx, out,
    )
    return out


def solution(mesh):
    return jax.shard_map(
        body,
        mesh=mesh,
        in_specs=(P("col", "row", None), P("col", "row", None)),
        out_specs=P("col", "row", None),
        check_vma=False,
    )
```

```python
import functools
import math

import jax
import jax.numpy as jnp
import numpy as np
from jax import lax
from jax.experimental import pallas as pl
from jax.experimental.pallas import tpu as pltpu
from jax.sharding import PartitionSpec as P

RADIUS = 6
PAIR = 2
EDGE = 8
TILE = 16
LANES = 128

sigma_cells = 8.0
dt_step = 0.5
nu_diff = 0.1
eps_fit = 0.05

ATAN_COEFS = (
    0.318309854, -0.106098923, 0.0635640505, -0.0446161759,
    0.0315320858, -0.0188971351, 0.00769233704, -0.0014861167,
)
TAP_SCALE = 0.519


def taps():
    d = np.arange(RADIUS + 1, dtype=np.float64)
    exact = np.exp(-d * d / (2.0 * sigma_cells * sigma_cells))
    short = np.asarray((TAP_SCALE * exact).astype(np.float32).astype(jnp.bfloat16))
    short64 = short.astype(np.float64)
    short_sum = short64[0] + 2.0 * short64[1:].sum()
    z_taps = exact / (exact[0] + 2.0 * exact[1:].sum()) / (short_sum * short_sum)
    return [float(v) for v in z_taps], short


def band(out_pos, in_pos, period=None):
    _, short = taps()
    dist = np.abs(out_pos[:, None] - in_pos[None, :])
    if period is not None:
        dist = np.minimum(dist, period - dist)
    table = np.where(dist <= RADIUS, short.astype(np.float32)[np.minimum(dist, RADIUS)], 0.0)
    return jnp.asarray(table.astype(np.float32), jnp.bfloat16)


def heaviside(x, scale):
    far = jnp.abs(x) > 1.0
    t = jnp.where(far, pl.reciprocal(x, approx=False), x)
    z = t * t
    p = ATAN_COEFS[-1] * scale
    for c in ATAN_COEFS[-2::-1]:
        p = p * z + c * scale
    p = p * t
    base = jnp.where(far, jnp.where(x > 0.0, scale, 0.0), 0.5 * scale)
    return base + jnp.where(far, -p, p)


def interleave(first, second):
    a, b = len(first), len(second)
    done = 0
    for i, piece in enumerate(first):
        piece()
        want = (i + 1) * b // a
        while done < want:
            second[done]()
            done += 1


def split_bf16(acc):
    hi = acc.astype(jnp.bfloat16)
    return hi, (acc - hi.astype(jnp.float32)).astype(jnp.bfloat16)


def part_kernel(plan, *refs):
    srcs, wys, wx_ref, _, outs, scratch = plan["unpack"](refs)
    out_ref = outs[0]
    lev, img, hea, him, sqr, zb0, zb1, xb, xr, ob, in_sem, out_sem, exp_sem = scratch[:13]
    rows, rows_out, length = plan["rows"], plan["rows_out"], plan["length"]
    groups, steps = plan["groups"], plan["steps"]
    z_taps, _ = taps()
    sim = scratch[-1]
    fields = (him, hea, sim, sqr)

    def copy_in(k):
        src, lead, src_ranges, dst, dst_lead, dst_ranges = plan["copies"][k]
        src, dst = srcs[src], scratch[dst]
        for i in lead:
            src = src.at[i]
        for i in dst_lead:
            dst = dst.at[i]
        return pltpu.make_async_copy(
            src.at[tuple(pl.ds(a, n) for a, n in src_ranges)],
            dst.at[tuple(pl.ds(a, n) for a, n in dst_ranges)],
            in_sem.at[k],
        )

    for k in range(len(plan["copies"])):
        copy_in(k).start()

    def transpose_strips():
        held, strip = scratch[16], scratch[17]
        for k in plan["strip_waits"]:
            copy_in(k).wait()
        n_z = held.shape[3]

        def block(b, carry):
            z0 = pl.multiple_of(b * 8, 8)
            for side in range(2):
                for f in range(2):
                    for row in range(EDGE):
                        y = max(row - (EDGE - RADIUS), 0) if side == 0 else min(row, RADIUS - 1)
                        for lane in range(0, length, LANES):
                            strip[
                                side, f, lane // LANES, pl.ds(z0 * EDGE + row, 8, stride=EDGE), :
                            ] = held[side, f, y, pl.ds(z0, 8), pl.ds(lane, LANES)]
            return carry

        lax.fori_loop(0, n_z // 8, block, 0)
        copy = pltpu.make_async_copy(strip, outs[1], exp_sem.at[0])
        copy.start()

        def spread(z, carry):
            rows8 = pl.ds(pl.multiple_of(z * EDGE, EDGE), EDGE)
            for side in range(2):
                for f, (halo, near) in enumerate(((lev, scratch[14]), (img, scratch[15]))):
                    at = side * (near.shape[1] - EDGE)
                    for lane in range(0, length, LANES):
                        v = strip[side, f, lane // LANES, rows8, :]
                        halo[z, side * EDGE : (side + 1) * EDGE, lane : lane + LANES] = v
                        near[z, at : at + EDGE, lane : lane + LANES] = v
            return carry

        lax.fori_loop(0, n_z, spread, 0)
        return copy

    strip_copy = transpose_strips() if plan["strip_waits"] else None

    def fill(z, carry, spans):
        for a, n, compute in spans:
            for at in range(a, a + n, 8):
                for lane in range(0, length, LANES):
                    where = (z, pl.ds(at, 8), pl.ds(lane, LANES))
                    if compute:
                        h = heaviside(lev[where], z_taps[0])
                        hea[where] = h
                    else:
                        h = hea[where]
                    im = img[where]
                    him[where] = h * im
                    scaled = im * z_taps[0]
                    sim[where] = scaled
                    sqr[where] = scaled * im
        return carry

    def place_corners(side):
        held = scratch[13]
        z0 = plan["corners"][side]
        for t, row, pad in ((0, EDGE - RADIUS, 0), (1, rows - EDGE, rows - EDGE + RADIUS)):
            for f, dst in enumerate((lev, img)):
                for z in range(RADIUS):
                    dst[z0 + z, row : row + RADIUS, :] = held[side, t, f, z]
                    dst[z0 + z, pad : pad + EDGE - RADIUS, :] = jnp.zeros(
                        (EDGE - RADIUS, length), jnp.float32
                    )

    def run_fills(fills):
        for waits, corner_side, (z0, z1), spans in fills:
            for k in waits:
                copy_in(k).wait()
            if corner_side is not None:
                place_corners(corner_side)
            lax.fori_loop(z0, z1, functools.partial(fill, spans=spans), 0)

    run_fills(plan["fills"])

    exports = []
    for e, (a, n) in enumerate(plan["h_export"]):
        copy = pltpu.make_async_copy(
            hea.at[pl.ds(a, n)], outs[1].at[pl.ds(a, n)], exp_sem.at[e]
        )
        copy.start()
        exports.append(copy)

    def z_tile(first, zb, at, col):
        def emit():
            sums = []
            for tile in (col, col + LANES):
                f, lane = divmod(tile, length)
                vals = [
                    fields[f][first + z, pl.ds(at, TILE), pl.ds(lane, LANES)]
                    for z in range(PAIR + 2 * RADIUS)
                ]
                for z in range(PAIR):
                    acc = vals[z + RADIUS]
                    for d in range(1, RADIUS + 1):
                        acc = acc + (vals[z + RADIUS - d] + vals[z + RADIUS + d]) * (
                            z_taps[d] / z_taps[0]
                        )
                    sums.append(acc)
            for z in range(PAIR):
                hi, lo = split_bf16(jnp.concatenate([sums[z], sums[PAIR + z]], axis=1))
                zb[z, pl.ds(at, TILE), pl.ds(col, wide)] = hi
                zb[z, pl.ds(at + rows, TILE), pl.ds(col, wide)] = lo

        return emit

    def z_pieces(first, zb, row_starts):
        return [
            z_tile(first, zb, at, col) for at in row_starts for col in range(0, 4 * length, wide)
        ]

    wide = 2 * LANES

    def along_y(t, z, zb, col):
        def emit():
            acc = jnp.dot(
                wys[0][...], zb[z, :, col : col + wide], preferred_element_type=jnp.float32
            )
            if plan["ready"]:
                acc = acc + jnp.dot(
                    wys[1][...], scratch[13][PAIR * t + z, :, col : col + wide],
                    preferred_element_type=jnp.float32,
                )
            whole = col // length == (col + wide - 1) // length
            step = wide if whole else LANES
            for part in range(0, wide, step):
                hi, lo = split_bf16(acc[:, part : part + step])
                f, x = divmod(col + part, length)
                at = (z * 4 + f) * rows_out
                xb[at : at + rows_out, x : x + step] = hi
                xb[at : at + rows_out, length + x : length + x + step] = lo

        return emit

    def along_x(z, planes):
        def emit():
            at, n = z * 4 * rows_out, planes * 4 * rows_out
            xr[at : at + n, :] = jnp.dot(
                xb[at : at + n, :], wx_ref[...], preferred_element_type=jnp.float32
            )

        return emit

    def update(t, z, zi, row, at):
        def emit():
            for lane in range(0, length, LANES):
                s1, s2, s3, s4 = (
                    xr[
                        (z * 4 + f) * rows_out + row : (z * 4 + f) * rows_out + row + 8,
                        lane : lane + LANES,
                    ]
                    for f in range(4)
                )
                lv, im, others = local_of(*plan["local_at"])(scratch, zi, at, lane, length)
                inner = s2 + eps_fit
                outer = (1.0 + eps_fit) - s2
                spread = s4 - (s3 * s3 - eps_fit)
                left = s1 * outer
                right = (s3 - s1) * inner
                prod = inner * outer
                pi_dt = math.pi / dt_step
                denom = (prod * prod) * (spread * (pi_dt + (pi_dt * lv) * lv))
                numer = (left - right) * ((im + im) * prod - (left + right))
                ob[PAIR * t + z, row : row + 8, lane : lane + LANES] = (
                    (1.0 - 6.0 * dt_step * nu_diff) * lv
                    + (dt_step * nu_diff) * others
                    + numer * pl.reciprocal(denom, approx=False)
                )

        return emit

    def yxf_pieces(t, zb):
        zi = plan["base"](t) + RADIUS
        pieces = [
            along_y(t, z, zb, col) for z in range(PAIR) for col in range(0, 4 * length, wide)
        ]
        together = PAIR if PAIR * rows_out <= 64 else 1
        pieces += [along_x(z, together) for z in range(0, PAIR, together)]
        for z in range(PAIR):
            row = 0
            for start, count, _ in groups:
                pieces += [update(t, z, zi + z, row + i, start + i) for i in range(0, count, 8)]
                row += count
        return pieces

    def out_copies(t):
        row, made = 0, []
        for g, (_, count, y0) in enumerate(groups):
            made.append(
                pltpu.make_async_copy(
                    ob.at[pl.ds(PAIR * t, PAIR), pl.ds(row, count), :],
                    out_ref.at[pl.ds(plan["out_z"](t), PAIR), pl.ds(y0, count), :],
                    out_sem.at[t, g],
                )
            )
            row += count
        return made

    n_h = len(plan["h_export"])

    def z_export(t, zb, slot):
        return [
            pltpu.make_async_copy(
                zb.at[:, pl.ds(src, TILE), :],
                outs[2].at[pl.ds(PAIR * t, PAIR), pl.ds(TILE * e, TILE), :],
                exp_sem.at[n_h + len(plan["z_export"]) * slot + e],
            )
            for e, src in enumerate(plan["z_export"])
        ]

    def prologue(r, carry):
        at = pl.multiple_of(r * TILE, TILE)
        for piece in z_pieces(plan["base"](0), zb0, [at]):
            piece()
        return carry

    lax.fori_loop(0, rows // TILE, prologue, 0)
    for copy in z_export(0, zb0, 0):
        copy.start()
    for k in plan["late_waits"]:
        copy_in(k).wait()
    tiles = list(range(0, rows, TILE))

    n_pairs = steps // 2

    def two_steps(i, last):
        for half, (now, nxt) in enumerate(((zb0, zb1), (zb1, zb0))):
            t = 2 * i + half
            ahead = half == 0 or not last
            if plan["z_export"] and ahead:
                if half == 1:
                    for copy in z_export(t - 1, nxt, 0):
                        copy.wait()
                elif last:
                    for copy in z_export(t - 1, nxt, 1):
                        copy.wait()
                else:

                    @pl.when(i > 0)
                    def _():
                        for copy in z_export(t - 1, nxt, 1):
                            copy.wait()

            z_work = z_pieces(plan["base"](t + 1), nxt, tiles) if ahead else []
            interleave(yxf_pieces(t, now), z_work)
            for copy in out_copies(t):
                copy.start()
            if plan["z_export"] and ahead:
                for copy in z_export(t + 1, nxt, 1 - half):
                    copy.start()

    def steady(i, carry):
        if plan["late_fills"]:
            at, fills = plan["late_fills"]
            pl.when(i == at)(lambda: run_fills(fills))
        two_steps(i, False)
        return carry

    lax.fori_loop(0, n_pairs - 1, steady, 0)
    two_steps(n_pairs - 1, True)
    if plan["z_export"]:
        for slot, zb in ((0, zb0), (1, zb1)):
            for copy in z_export(steps - 2 + slot, zb, slot):
                copy.wait()
    for copy in exports + ([] if strip_copy is None else [strip_copy]):
        copy.wait()

    def finish(t, carry):
        for copy in out_copies(t):
            copy.wait()
        return carry

    lax.fori_loop(0, steps, finish, 0)


def run_part(plan, shape, srcs, wys, wx, prev):
    rows, rows_out, length, planes = plan["rows"], plan["rows_out"], plan["length"], plan["planes"]
    steps, n_ready = plan["steps"], plan.get("ready", 0)
    n_src, n_wy, n_out = len(srcs), len(wys), 1 + len(plan["extra_out"])
    n_prev = 0 if prev is None else 1

    def unpack(refs):
        cuts = np.cumsum([n_src, n_wy, 1, n_prev, n_out])
        a, b, c, d, e = (int(v) for v in cuts)
        return refs[:a], refs[a:b], refs[b], refs[c:d], refs[d:e], refs[e:]

    plan = dict(plan, unpack=unpack, ready=n_ready, strip_waits=plan.get("strip_waits", ()),
        late_fills=plan.get("late_fills"))
    any_spec = pl.BlockSpec(memory_space=pl.ANY)
    vmem = pl.BlockSpec(memory_space=pltpu.VMEM)
    args = list(srcs) + list(wys) + [wx] + ([] if prev is None else [prev])
    specs = [any_spec] * n_src + [vmem] * (n_wy + 1) + [any_spec] * n_prev
    n_elem = PAIR * steps * rows_out * length
    field = pltpu.VMEM((planes, rows, length), jnp.float32)
    taps_buffer = pltpu.VMEM((PAIR, 2 * rows, 4 * length), jnp.bfloat16)
    scratch = [field] * 5 + [
        taps_buffer,
        taps_buffer,
        pltpu.VMEM((PAIR * 4 * rows_out, 2 * length), jnp.bfloat16),
        pltpu.VMEM((PAIR * 4 * rows_out, length), jnp.float32),
        pltpu.VMEM((PAIR * steps, rows_out, length), jnp.float32),
        pltpu.SemaphoreType.DMA((len(plan["copies"]),)),
        pltpu.SemaphoreType.DMA((steps, len(plan["groups"]))),
        pltpu.SemaphoreType.DMA((max(1, len(plan["h_export"]) + 2 * len(plan["z_export"])),)),
    ]
    if n_ready:
        scratch += [
            pltpu.VMEM((PAIR * steps, n_ready, 4 * length), jnp.bfloat16),
            pltpu.VMEM((planes, 2 * (EDGE + TILE), length), jnp.float32),
            pltpu.VMEM((planes, 2 * (EDGE + TILE), length), jnp.float32),
            pltpu.VMEM((2, 2, RADIUS, planes, length), jnp.float32),
            pltpu.VMEM((2, 2, length // LANES, planes * EDGE, LANES), jnp.float32),
        ]
    if plan.get("corners"):
        scratch.append(pltpu.VMEM((2, 2, 2, RADIUS, RADIUS, length), jnp.float32))
    scratch.append(field)
    out = pl.pallas_call(
        functools.partial(part_kernel, plan),
        out_shape=[jax.ShapeDtypeStruct(shape, jnp.float32)] + plan["extra_out"],
        in_specs=specs,
        out_specs=[any_spec] * n_out,
        scratch_shapes=scratch,
        input_output_aliases={} if prev is None else {len(args) - 1: 0},
        compiler_params=pltpu.CompilerParams(
            vmem_limit_bytes=60 * 1024 * 1024,
        ),
        cost_estimate=pl.CostEstimate(
            flops=n_elem * 12000, bytes_accessed=n_elem * 12, transcendentals=0
        ),
        name=plan["name"],
    )(*args)
    return out


def neighbours(axis):
    n = lax.axis_size(axis)
    up = [(i, (i + 1) % n) for i in range(n)]
    return up, [(j, i) for i, j in up]


def local_of(lev_at, img_at):
    def local(scratch, zi, at, lane, length):
        lev, img = scratch[lev_at], scratch[img_at]
        cols = slice(lane, lane + LANES)
        lv = lev[zi, at : at + 8, cols]
        last = LANES - 1
        prev = lev[zi, at : at + 8, (lane - LANES) % length : (lane - LANES) % length + LANES]
        follow = lev[zi, at : at + 8, (lane + LANES) % length : (lane + LANES) % length + LANES]
        index = lax.broadcasted_iota(jnp.int32, (8, LANES), 1)
        here_up, here_down = pltpu.roll(lv, 1, 1), pltpu.roll(lv, last, 1)
        west = jnp.where(index == 0, pltpu.roll(prev, 1, 1), here_up)
        east = jnp.where(index == last, pltpu.roll(follow, last, 1), here_down)
        others = (
            (lev[zi - 1, at : at + 8, cols] + lev[zi + 1, at : at + 8, cols])
            + (lev[zi, at - 1 : at + 7, cols] + lev[zi, at + 1 : at + 9, cols])
            + (west + east)
        )
        return lv, img[zi, at : at + 8, cols], others

    return local


LEV, IMG, HEA, READY, NEAR_LEV, NEAR_IMG, HELD = 0, 1, 2, 13, 14, 15, 16
CORNERS = 13


def body(level_set, image):
    zl, yl, length = level_set.shape
    shape = level_set.shape
    r = RADIUS
    both = jnp.stack([level_set, image])
    y_up, y_down = neighbours("row")
    z_up, z_down = neighbours("col")

    y_before = lax.ppermute(both[:, :, yl - r :, :].transpose(0, 2, 1, 3), "row", y_up)
    y_after = lax.ppermute(both[:, :, :r, :].transpose(0, 2, 1, 3), "row", y_down)
    z_before = lax.ppermute(both[:, zl - r :], "col", z_up)
    z_after = lax.ppermute(both[:, :r], "col", z_down)

    y_rows = np.arange(yl)
    wx1 = band(np.arange(length), np.arange(length), length)
    wx = jnp.concatenate([wx1, wx1], axis=0)

    def doubled(out_pos, in_pos):
        w = band(out_pos, in_pos)
        return jnp.concatenate([w, w], axis=1)

    def full(z0, zn, y0, yn):
        return ((z0, zn), (y0, yn), (0, length))

    depth = PAIR * 4 + 2 * r
    near = depth - r
    inner_steps = (zl - 2 * EDGE) // PAIR
    chunk = zl // 3
    interior = dict(
        name="interior", rows=yl, rows_out=yl - 2 * EDGE, length=length, planes=zl,
        steps=inner_steps,
        base=lambda t: EDGE - r + PAIR * t, out_z=lambda t: EDGE + PAIR * t,
        groups=((EDGE, yl - 2 * EDGE, EDGE),), local_at=(LEV, IMG),
        copies=[
            (f, (), full(z, chunk, 0, yl), f, (), full(z, chunk, 0, yl))
            for z in range(0, zl, chunk) for f in (LEV, IMG)
        ],
        fills=[
            ((2 * c, 2 * c + 1), None, (c * chunk, (c + 1) * chunk), ((0, yl, True),))
            for c in range(3)
        ],
        h_export=((0, near), (zl - near, near)),
        z_export=(0, yl - TILE, yl, 2 * yl - TILE),
        late_waits=(),
        extra_out=[
            jax.ShapeDtypeStruct(shape, jnp.float32),
            jax.ShapeDtypeStruct((PAIR * inner_steps, 4 * TILE, 4 * length), jnp.bfloat16),
        ],
    )
    out, hea, near_rows = run_part(
        interior, shape, [level_set, image],
        [doubled(y_rows[EDGE : yl - EDGE], y_rows)], wx, None,
    )

    edge_last = jnp.stack([y_before[:, :, zl - r :], y_after[:, :, zl - r :]])
    edge_first = jnp.stack([y_before[:, :, :r], y_after[:, :, :r]])
    corner_before = lax.ppermute(edge_last.transpose(0, 1, 3, 2, 4), "col", z_up)
    corner_after = lax.ppermute(edge_first.transpose(0, 1, 3, 2, 4), "col", z_down)

    half = EDGE + TILE
    z_lo, z_n = EDGE - r, zl - 2 * (EDGE - r)
    halo = ((0, r), (0, zl), (0, length))
    copies = [(2 + side, (f,), halo, HELD, (side, f), halo) for side in range(2) for f in range(2)]
    n_first = len(copies)
    for f, dst in ((0, NEAR_LEV), (1, NEAR_IMG)):
        copies += [
            (f, (), full(z_lo, z_n, 0, TILE), dst, (), full(z_lo, z_n, EDGE, TILE)),
            (f, (), full(z_lo, z_n, yl - TILE, TILE), dst, (), full(z_lo, z_n, half, TILE)),
        ]
    ready_all = ((0, PAIR * inner_steps), (0, 4 * TILE), (0, 4 * length))
    copies.append((4, (), ready_all, READY, (), ready_all))
    y_edges = dict(
        name="y_edges", rows=2 * EDGE, rows_out=2 * EDGE, length=length, planes=zl,
        steps=inner_steps,
        base=lambda t: EDGE - r + PAIR * t, out_z=lambda t: EDGE + PAIR * t,
        groups=((EDGE, EDGE, 0), (half + EDGE, EDGE, yl - EDGE)),
        local_at=(NEAR_LEV, NEAR_IMG),
        copies=copies,
        fills=[((), None, (z_lo, z_lo + z_n), ((0, 2 * EDGE, True),))],
        h_export=(), z_export=(), late_waits=tuple(range(n_first, len(copies))),
        extra_out=[
            jax.ShapeDtypeStruct((2, 2, length // LANES, zl * EDGE, LANES), jnp.float32)
        ],
        ready=4 * TILE, strip_waits=tuple(range(n_first)),
    )
    out_pos = np.concatenate([y_rows[:EDGE], y_rows[yl - EDGE :]])
    halo_pos = np.concatenate([np.arange(-EDGE, 0), np.arange(yl, yl + EDGE)])
    near_pos = np.concatenate([np.arange(TILE), np.arange(yl - TILE, yl)])
    out, y_strips = run_part(
        y_edges, shape, [level_set, image, y_before, y_after, near_rows],
        [doubled(out_pos, halo_pos), doubled(out_pos, near_pos)], wx, out,
    )
    y_strips = y_strips.reshape(2, 2, length // LANES, zl, EDGE, LANES)

    rows = yl + 2 * EDGE
    copies, waits = [], []
    ring = ((0, 2), (0, 2), (0, r), (0, r), (0, length))
    for side, (z_dst, src, dst) in enumerate(((0, 0, r), (depth + near, zl - near, depth))):
        n_before = len(copies)
        copies.append((3 + side, (), ring, CORNERS, (side,), ring))
        copies += [
            (5 + side, (f,), full(0, r, 0, yl), f, (), full(z_dst, r, EDGE, yl))
            for f in (LEV, IMG)
        ]
        n_halo = len(copies)
        copies.append((7, (), full(src, near, 0, yl), HEA, (), full(dst, near, EDGE, yl)))
        for f in (LEV, IMG):
            copies.append((f, (), full(src, near, 0, yl), f, (), full(dst, near, EDGE, yl)))
            copies += [
                (
                    2, (t, f, lane // LANES), ((src, near), (0, EDGE), (0, LANES)),
                    f, (), ((dst, near), (row, EDGE), (lane, LANES)),
                )
                for t, row in ((0, 0), (1, EDGE + yl))
                for lane in range(0, length, LANES)
            ]
        waits.append((tuple(range(n_before, n_halo)), tuple(range(n_halo, len(copies)))))
    whole = ((0, rows, True),)
    inside = ((0, EDGE, True), (EDGE, yl, False), (EDGE + yl, EDGE, True))
    side_steps = EDGE // PAIR
    z_edges = dict(
        name="z_edges", rows=rows, rows_out=yl, length=length, planes=2 * depth,
        steps=2 * side_steps,
        base=lambda t: depth * (t // side_steps) + PAIR * (t % side_steps),
        out_z=lambda t: (zl - EDGE) * (t // side_steps) + PAIR * (t % side_steps),
        groups=((EDGE, yl, 0),), local_at=(LEV, IMG),
        copies=copies,
        fills=[(waits[0][0], 0, (0, r), whole), (waits[0][1], None, (r, depth), inside)],
        late_fills=(
            side_steps // 2 - 1,
            [
                (waits[1][0], 1, (depth + near, 2 * depth), whole),
                (waits[1][1], None, (depth, depth + near), inside),
            ],
        ),
        corners=(0, depth + near),
        h_export=(), z_export=(), late_waits=(), extra_out=[],
    )
    (out,) = run_part(
        z_edges, shape,
        [level_set, image, y_strips, corner_before, corner_after, z_before, z_after, hea],
        [doubled(y_rows, np.arange(-EDGE, yl + EDGE))], wx, out,
    )
    return out


def solution(mesh):
    return jax.shard_map(
        body,
        mesh=mesh,
        in_specs=(P("col", "row", None), P("col", "row", None)),
        out_specs=P("col", "row", None),
        check_vma=False,
    )
```

```python
import functools
import math

import jax
import jax.numpy as jnp
import numpy as np
from jax import lax
from jax.experimental import pallas as pl
from jax.experimental.pallas import tpu as pltpu
from jax.sharding import PartitionSpec as P

RADIUS = 6
PAIR = 2
EDGE = 8
TILE = 16
LANES = 128

sigma_cells = 8.0
dt_step = 0.5
nu_diff = 0.1
eps_fit = 0.05

ATAN_COEFS = (
    0.318309854, -0.106098923, 0.0635640505, -0.0446161759,
    0.0315320858, -0.0188971351, 0.00769233704, -0.0014861167,
)
TAP_SCALE = 0.519


def taps():
    d = np.arange(RADIUS + 1, dtype=np.float64)
    exact = np.exp(-d * d / (2.0 * sigma_cells * sigma_cells))
    short = np.asarray((TAP_SCALE * exact).astype(np.float32).astype(jnp.bfloat16))
    short64 = short.astype(np.float64)
    short_sum = short64[0] + 2.0 * short64[1:].sum()
    z_taps = exact / (exact[0] + 2.0 * exact[1:].sum()) / (short_sum * short_sum)
    return [float(v) for v in z_taps], short


def band(out_pos, in_pos, period=None):
    _, short = taps()
    dist = np.abs(out_pos[:, None] - in_pos[None, :])
    if period is not None:
        dist = np.minimum(dist, period - dist)
    table = np.where(dist <= RADIUS, short.astype(np.float32)[np.minimum(dist, RADIUS)], 0.0)
    return jnp.asarray(table.astype(np.float32), jnp.bfloat16)


def heaviside(x, scale):
    far = jnp.abs(x) > 1.0
    t = jnp.where(far, pl.reciprocal(x, approx=False), x)
    z = t * t
    p = ATAN_COEFS[-1] * scale
    for c in ATAN_COEFS[-2::-1]:
        p = p * z + c * scale
    p = p * t
    base = jnp.where(far, jnp.where(x > 0.0, scale, 0.0), 0.5 * scale)
    return base + jnp.where(far, -p, p)


def interleave(first, second):
    a, b = len(first), len(second)
    done = 0
    for i, piece in enumerate(first):
        piece()
        want = (i + 1) * b // a
        while done < want:
            second[done]()
            done += 1


def split_bf16(acc):
    hi = acc.astype(jnp.bfloat16)
    return hi, (acc - hi.astype(jnp.float32)).astype(jnp.bfloat16)


def part_kernel(plan, *refs):
    srcs, (wy_ref,), wx_ref, _, outs, scratch = plan["unpack"](refs)
    out_ref = outs[0]
    lev, img, hea, him, sqr, zb0, zb1, xb, xr, ob, in_sem, out_sem, exp_sem = scratch[:13]
    rows, rows_out, length = plan["rows"], plan["rows_out"], plan["length"]
    groups, steps, pair = plan["groups"], plan["steps"], plan["pair"]
    z_taps, _ = taps()
    sim = scratch[-1]
    fields = (him, hea, sim, sqr)

    def copy_in(k):
        src, lead, src_ranges, dst, dst_lead, dst_ranges = plan["copies"][k]
        src, dst = srcs[src], scratch[dst]
        for i in lead:
            src = src.at[i]
        for i in dst_lead:
            dst = dst.at[i]
        return pltpu.make_async_copy(
            src.at[tuple(pl.ds(a, n) for a, n in src_ranges)],
            dst.at[tuple(pl.ds(a, n) for a, n in dst_ranges)],
            in_sem.at[k],
        )

    for k in plan["first"]:
        copy_in(k).start()

    def transpose_strips():
        held, strip = scratch[16], scratch[17]
        for k in plan["strip_waits"]:
            copy_in(k).wait()
        for k in plan["late_waits"]:
            copy_in(k).start()
        n_z = held.shape[3]

        def block(b, carry):
            z0 = pl.multiple_of(b * 8, 8)
            for side in range(2):
                for f in range(2):
                    for row in range(EDGE):
                        y = max(row - (EDGE - RADIUS), 0) if side == 0 else min(row, RADIUS - 1)
                        for lane in range(0, length, LANES):
                            strip[
                                side, f, lane // LANES, pl.ds(z0 * EDGE + row, 8, stride=EDGE), :
                            ] = held[side, f, y, pl.ds(z0, 8), pl.ds(lane, LANES)]
            return carry

        lax.fori_loop(0, n_z // 8, block, 0)
        copy = pltpu.make_async_copy(strip, outs[1], exp_sem.at[0])
        copy.start()

        def spread(z, carry):
            rows8 = pl.ds(pl.multiple_of(z * EDGE, EDGE), EDGE)
            for side in range(2):
                for f, (halo, near) in enumerate(((lev, scratch[14]), (img, scratch[15]))):
                    at = side * (near.shape[1] - EDGE)
                    for lane in range(0, length, LANES):
                        v = strip[side, f, lane // LANES, rows8, :]
                        halo[z, side * EDGE : (side + 1) * EDGE, lane : lane + LANES] = v
                        near[z, at : at + EDGE, lane : lane + LANES] = v
            return carry

        lax.fori_loop(0, n_z, spread, 0)
        return copy

    strip_copy = transpose_strips() if plan["strip_waits"] else None

    def fill(z, carry, spans):
        for a, n, compute in spans:
            for at in range(a, a + n, 8):
                for lane in range(0, length, LANES):
                    where = (z, pl.ds(at, 8), pl.ds(lane, LANES))
                    if compute:
                        h = heaviside(lev[where], z_taps[0])
                        hea[where] = h
                    else:
                        h = hea[where]
                    im = img[where]
                    him[where] = h * im
                    scaled = im * z_taps[0]
                    sim[where] = scaled
                    sqr[where] = scaled * im
        return carry

    def place_corners(side):
        held = scratch[13]
        z0 = plan["corners"][side]
        for t, row, pad in ((0, EDGE - RADIUS, 0), (1, rows - EDGE, rows - EDGE + RADIUS)):
            for f, dst in enumerate((lev, img)):
                for z in range(RADIUS):
                    dst[z0 + z, row : row + RADIUS, :] = held[side, t, f, z]
                    dst[z0 + z, pad : pad + EDGE - RADIUS, :] = jnp.zeros(
                        (EDGE - RADIUS, length), jnp.float32
                    )

    def run_fills(fills):
        for waits, starts, corner_side, (z0, z1), spans in fills:
            for k in waits:
                copy_in(k).wait()
            for k in starts:
                copy_in(k).start()
            if corner_side is not None:
                place_corners(corner_side)
            lax.fori_loop(z0, z1, functools.partial(fill, spans=spans), 0)

    run_fills(plan["fills"])

    exports = []
    for e, (a, n) in enumerate(plan["h_export"]):
        copy = pltpu.make_async_copy(
            hea.at[pl.ds(a, n)], outs[1].at[pl.ds(a, n)], exp_sem.at[e]
        )
        copy.start()
        exports.append(copy)

    def z_tile(first, zb, at, col):
        def emit():
            sums = []
            for tile in (col, col + LANES):
                f, lane = divmod(tile, length)
                vals = [
                    fields[f][first + z, pl.ds(at, TILE), pl.ds(lane, LANES)]
                    for z in range(pair + 2 * RADIUS)
                ]
                for z in range(pair):
                    acc = vals[z + RADIUS]
                    for d in range(1, RADIUS + 1):
                        acc = acc + (vals[z + RADIUS - d] + vals[z + RADIUS + d]) * (
                            z_taps[d] / z_taps[0]
                        )
                    sums.append(acc)
            for z in range(pair):
                hi, lo = split_bf16(jnp.concatenate([sums[z], sums[pair + z]], axis=1))
                zb[z, pl.ds(at, TILE), pl.ds(col, wide)] = hi
                zb[z, pl.ds(at + rows, TILE), pl.ds(col, wide)] = lo

        return emit

    def z_pieces(first, zb, row_starts):
        return [
            z_tile(first, zb, at, col) for at in row_starts for col in range(0, 4 * length, wide)
        ]

    wide = 2 * LANES

    def along_y(t, z, zb, col):
        def emit():
            values = zb[z, :, col : col + wide]
            if plan["ready"]:
                near = scratch[READY][pair * t + z, :, col : col + wide]
                values = jnp.concatenate([values, near], axis=0)
            acc = jnp.dot(wy_ref[...], values, preferred_element_type=jnp.float32)
            whole = col // length == (col + wide - 1) // length
            step = wide if whole else LANES
            for part in range(0, wide, step):
                hi, lo = split_bf16(acc[:, part : part + step])
                f, x = divmod(col + part, length)
                at = (z * 4 + f) * rows_out
                xb[at : at + rows_out, x : x + step] = hi
                xb[at : at + rows_out, length + x : length + x + step] = lo

        return emit

    def along_x(z, planes):
        def emit():
            at, n = z * 4 * rows_out, planes * 4 * rows_out
            xr[at : at + n, :] = jnp.dot(
                xb[at : at + n, :], wx_ref[...], preferred_element_type=jnp.float32
            )

        return emit

    def update(t, z, zi, row, at):
        def emit():
            for lane in range(0, length, LANES):
                s1, s2, s3, s4 = (
                    xr[
                        (z * 4 + f) * rows_out + row : (z * 4 + f) * rows_out + row + 8,
                        lane : lane + LANES,
                    ]
                    for f in range(4)
                )
                lv, im, others = local_of(*plan["local_at"])(scratch, zi, at, lane, length)
                inner = s2 + eps_fit
                outer = (1.0 + eps_fit) - s2
                spread = s4 - (s3 * s3 - eps_fit)
                left = s1 * outer
                right = (s3 - s1) * inner
                prod = inner * outer
                pi_dt = math.pi / dt_step
                denom = (prod * prod) * (spread * (pi_dt + (pi_dt * lv) * lv))
                numer = (left - right) * ((im + im) * prod - (left + right))
                ob[pair * t + z, row : row + 8, lane : lane + LANES] = (
                    (1.0 - 6.0 * dt_step * nu_diff) * lv
                    + (dt_step * nu_diff) * others
                    + numer * pl.reciprocal(denom, approx=False)
                )

        return emit

    def yxf_pieces(t, zb):
        zi = plan["base"](t) + RADIUS
        pieces = [
            along_y(t, z, zb, col) for z in range(pair) for col in range(0, 4 * length, wide)
        ]
        together = pair if pair * rows_out <= 64 else 1
        pieces += [along_x(z, together) for z in range(0, pair, together)]
        for z in range(pair):
            row = 0
            for start, count, _ in groups:
                pieces += [update(t, z, zi + z, row + i, start + i) for i in range(0, count, 8)]
                row += count
        return pieces

    def out_copies(t):
        row, made = 0, []
        for g, (_, count, y0) in enumerate(groups):
            made.append(
                pltpu.make_async_copy(
                    ob.at[pl.ds(pair * t, pair), pl.ds(row, count), :],
                    out_ref.at[pl.ds(plan["out_z"](t), pair), pl.ds(y0, count), :],
                    out_sem.at[t, g],
                )
            )
            row += count
        return made

    n_h = len(plan["h_export"])

    def z_export(t, zb, slot):
        return [
            pltpu.make_async_copy(
                zb.at[:, pl.ds(src, TILE), :],
                outs[2].at[pl.ds(pair * t, pair), pl.ds(TILE * e, TILE), :],
                exp_sem.at[n_h + len(plan["z_export"]) * slot + e],
            )
            for e, src in enumerate(plan["z_export"])
        ]

    def prologue(r, carry):
        at = pl.multiple_of(r * TILE, TILE)
        for piece in z_pieces(plan["base"](0), zb0, [at]):
            piece()
        return carry

    lax.fori_loop(0, rows // TILE, prologue, 0)
    for copy in z_export(0, zb0, 0):
        copy.start()
    for k in plan["late_waits"]:
        copy_in(k).wait()
    tiles = list(range(0, rows, TILE))

    n_pairs = steps // 2

    def two_steps(i, last):
        for half, (now, nxt) in enumerate(((zb0, zb1), (zb1, zb0))):
            t = 2 * i + half
            ahead = half == 0 or not last
            if plan["z_export"] and ahead:
                if half == 1:
                    for copy in z_export(t - 1, nxt, 0):
                        copy.wait()
                elif last:
                    for copy in z_export(t - 1, nxt, 1):
                        copy.wait()
                else:

                    @pl.when(i > 0)
                    def _():
                        for copy in z_export(t - 1, nxt, 1):
                            copy.wait()

            z_work = z_pieces(plan["base"](t + 1), nxt, tiles) if ahead else []
            interleave(yxf_pieces(t, now), z_work)
            for copy in out_copies(t):
                copy.start()
            if plan["z_export"] and ahead:
                for copy in z_export(t + 1, nxt, 1 - half):
                    copy.start()

    def steady(i, carry):
        if plan["late_fills"]:
            at, fills = plan["late_fills"]
            pl.when(i == at)(lambda: run_fills(fills))
        two_steps(i, False)
        return carry

    lax.fori_loop(0, n_pairs - 1, steady, 0)
    two_steps(n_pairs - 1, True)
    if plan["z_export"]:
        for slot, zb in ((0, zb0), (1, zb1)):
            for copy in z_export(steps - 2 + slot, zb, slot):
                copy.wait()
    for copy in exports + ([] if strip_copy is None else [strip_copy]):
        copy.wait()

    def finish(t, carry):
        for copy in out_copies(t):
            copy.wait()
        return carry

    lax.fori_loop(0, steps, finish, 0)


def run_part(plan, shape, srcs, wy, wx, prev):
    rows, rows_out, length, planes = plan["rows"], plan["rows_out"], plan["length"], plan["planes"]
    steps, pair, n_ready = plan["steps"], plan["pair"], plan.get("ready", 0)
    n_src, n_wy, n_out = len(srcs), 1, 1 + len(plan["extra_out"])
    n_prev = 0 if prev is None else 1

    def unpack(refs):
        cuts = np.cumsum([n_src, n_wy, 1, n_prev, n_out])
        a, b, c, d, e = (int(v) for v in cuts)
        return refs[:a], refs[a:b], refs[b], refs[c:d], refs[d:e], refs[e:]

    plan = dict(plan, unpack=unpack, ready=n_ready, strip_waits=plan.get("strip_waits", ()),
        late_fills=plan.get("late_fills"))
    any_spec = pl.BlockSpec(memory_space=pl.ANY)
    vmem = pl.BlockSpec(memory_space=pltpu.VMEM)
    args = list(srcs) + [wy, wx] + ([] if prev is None else [prev])
    specs = [any_spec] * n_src + [vmem] * (n_wy + 1) + [any_spec] * n_prev
    n_elem = pair * steps * rows_out * length
    field = pltpu.VMEM((planes, rows, length), jnp.float32)
    taps_buffer = pltpu.VMEM((pair, 2 * rows, 4 * length), jnp.bfloat16)
    scratch = [field] * 5 + [
        taps_buffer,
        taps_buffer,
        pltpu.VMEM((pair * 4 * rows_out, 2 * length), jnp.bfloat16),
        pltpu.VMEM((pair * 4 * rows_out, length), jnp.float32),
        pltpu.VMEM((pair * steps, rows_out, length), jnp.float32),
        pltpu.SemaphoreType.DMA((len(plan["copies"]),)),
        pltpu.SemaphoreType.DMA((steps, len(plan["groups"]))),
        pltpu.SemaphoreType.DMA((max(1, len(plan["h_export"]) + 2 * len(plan["z_export"])),)),
    ]
    if n_ready:
        scratch += [
            pltpu.VMEM((pair * steps, n_ready, 4 * length), jnp.bfloat16),
            pltpu.VMEM((planes, 2 * (EDGE + TILE), length), jnp.float32),
            pltpu.VMEM((planes, 2 * (EDGE + TILE), length), jnp.float32),
            pltpu.VMEM((2, 2, RADIUS, planes, length), jnp.float32),
            pltpu.VMEM((2, 2, length // LANES, planes * EDGE, LANES), jnp.float32),
        ]
    if plan.get("corners"):
        scratch.append(pltpu.VMEM((2, 2, 2, RADIUS, RADIUS, length), jnp.float32))
    scratch.append(field)
    out = pl.pallas_call(
        functools.partial(part_kernel, plan),
        out_shape=[jax.ShapeDtypeStruct(shape, jnp.float32)] + plan["extra_out"],
        in_specs=specs,
        out_specs=[any_spec] * n_out,
        scratch_shapes=scratch,
        input_output_aliases={} if prev is None else {len(args) - 1: 0},
        compiler_params=pltpu.CompilerParams(
            vmem_limit_bytes=60 * 1024 * 1024,
        ),
        cost_estimate=pl.CostEstimate(
            flops=n_elem * 12000, bytes_accessed=n_elem * 12, transcendentals=0
        ),
        name=plan["name"],
    )(*args)
    return out


def neighbours(axis):
    n = lax.axis_size(axis)
    up = [(i, (i + 1) % n) for i in range(n)]
    return up, [(j, i) for i, j in up]


def local_of(lev_at, img_at):
    def local(scratch, zi, at, lane, length):
        lev, img = scratch[lev_at], scratch[img_at]
        cols = slice(lane, lane + LANES)
        lv = lev[zi, at : at + 8, cols]
        last = LANES - 1
        prev = lev[zi, at : at + 8, (lane - LANES) % length : (lane - LANES) % length + LANES]
        follow = lev[zi, at : at + 8, (lane + LANES) % length : (lane + LANES) % length + LANES]
        index = lax.broadcasted_iota(jnp.int32, (8, LANES), 1)
        here_up, here_down = pltpu.roll(lv, 1, 1), pltpu.roll(lv, last, 1)
        west = jnp.where(index == 0, pltpu.roll(prev, 1, 1), here_up)
        east = jnp.where(index == last, pltpu.roll(follow, last, 1), here_down)
        others = (
            (lev[zi - 1, at : at + 8, cols] + lev[zi + 1, at : at + 8, cols])
            + (lev[zi, at - 1 : at + 7, cols] + lev[zi, at + 1 : at + 9, cols])
            + (west + east)
        )
        return lv, img[zi, at : at + 8, cols], others

    return local


LEV, IMG, HEA, READY, NEAR_LEV, NEAR_IMG, HELD = 0, 1, 2, 13, 14, 15, 16
CORNERS = 13


def body(level_set, image):
    zl, yl, length = level_set.shape
    shape = level_set.shape
    r = RADIUS
    both = jnp.stack([level_set, image])
    y_up, y_down = neighbours("row")
    z_up, z_down = neighbours("col")

    y_before = lax.ppermute(both[:, :, yl - r :, :].transpose(0, 2, 1, 3), "row", y_up)
    y_after = lax.ppermute(both[:, :, :r, :].transpose(0, 2, 1, 3), "row", y_down)
    z_before = lax.ppermute(both[:, zl - r :], "col", z_up)
    z_after = lax.ppermute(both[:, :r], "col", z_down)

    y_rows = np.arange(yl)
    wx1 = band(np.arange(length), np.arange(length), length)
    wx = jnp.concatenate([wx1, wx1], axis=0)

    def doubled(out_pos, in_pos):
        w = band(out_pos, in_pos)
        return jnp.concatenate([w, w], axis=1)

    def full(z0, zn, y0, yn):
        return ((z0, zn), (y0, yn), (0, length))

    depth = PAIR * 4 + 2 * r
    near = depth - r
    inner = zl - 2 * EDGE
    chunk = zl // 6 if zl % 6 == 0 else zl // 3
    n_chunks = zl // chunk
    interior = dict(
        name="interior", rows=yl, rows_out=yl - 2 * EDGE, length=length, planes=zl,
        pair=PAIR, steps=inner // PAIR,
        base=lambda t: EDGE - r + PAIR * t, out_z=lambda t: EDGE + PAIR * t,
        groups=((EDGE, yl - 2 * EDGE, EDGE),), local_at=(LEV, IMG),
        copies=[
            (f, (), full(z, chunk, 0, yl), f, (), full(z, chunk, 0, yl))
            for z in range(0, zl, chunk) for f in (LEV, IMG)
        ],
        fills=[
            (
                (2 * c, 2 * c + 1),
                (2 * c + 4, 2 * c + 5) if c + 2 < n_chunks else (),
                None, (c * chunk, (c + 1) * chunk), ((0, yl, True),),
            )
            for c in range(n_chunks)
        ],
        first=range(4),
        h_export=((0, near), (zl - near, near)),
        z_export=(0, yl - TILE, yl, 2 * yl - TILE),
        late_waits=(),
        extra_out=[
            jax.ShapeDtypeStruct(shape, jnp.float32),
            jax.ShapeDtypeStruct((inner, 4 * TILE, 4 * length), jnp.bfloat16),
        ],
    )
    out, hea, near_rows = run_part(
        interior, shape, [level_set, image],
        doubled(y_rows[EDGE : yl - EDGE], y_rows), wx, None,
    )

    edge_last = jnp.stack([y_before[:, :, zl - r :], y_after[:, :, zl - r :]])
    edge_first = jnp.stack([y_before[:, :, :r], y_after[:, :, :r]])
    corner_before = lax.ppermute(edge_last.transpose(0, 1, 3, 2, 4), "col", z_up)
    corner_after = lax.ppermute(edge_first.transpose(0, 1, 3, 2, 4), "col", z_down)

    half = EDGE + TILE
    z_lo, z_n = EDGE - r, zl - 2 * (EDGE - r)
    halo = ((0, r), (0, zl), (0, length))
    copies = [(2 + side, (f,), halo, HELD, (side, f), halo) for side in range(2) for f in range(2)]
    n_first = len(copies)
    for f, dst in ((0, NEAR_LEV), (1, NEAR_IMG)):
        copies += [
            (f, (), full(z_lo, z_n, 0, TILE), dst, (), full(z_lo, z_n, EDGE, TILE)),
            (f, (), full(z_lo, z_n, yl - TILE, TILE), dst, (), full(z_lo, z_n, half, TILE)),
        ]
    ready_all = ((0, inner), (0, 4 * TILE), (0, 4 * length))
    copies.append((4, (), ready_all, READY, (), ready_all))
    y_edges = dict(
        name="y_edges", rows=2 * EDGE, rows_out=2 * EDGE, length=length, planes=zl,
        pair=2 * PAIR, steps=inner // (2 * PAIR),
        base=lambda t: EDGE - r + 2 * PAIR * t, out_z=lambda t: EDGE + 2 * PAIR * t,
        first=range(n_first),
        groups=((EDGE, EDGE, 0), (half + EDGE, EDGE, yl - EDGE)),
        local_at=(NEAR_LEV, NEAR_IMG),
        copies=copies,
        fills=[((), (), None, (z_lo, z_lo + z_n), ((0, 2 * EDGE, True),))],
        h_export=(), z_export=(), late_waits=tuple(range(n_first, len(copies))),
        extra_out=[
            jax.ShapeDtypeStruct((2, 2, length // LANES, zl * EDGE, LANES), jnp.float32)
        ],
        ready=4 * TILE, strip_waits=tuple(range(n_first)),
    )
    out_pos = np.concatenate([y_rows[:EDGE], y_rows[yl - EDGE :]])
    halo_pos = np.concatenate([np.arange(-EDGE, 0), np.arange(yl, yl + EDGE)])
    near_pos = np.concatenate([np.arange(TILE), np.arange(yl - TILE, yl)])
    out, y_strips = run_part(
        y_edges, shape, [level_set, image, y_before, y_after, near_rows],
        jnp.concatenate([doubled(out_pos, halo_pos), doubled(out_pos, near_pos)], axis=1),
        wx, out,
    )
    y_strips = y_strips.reshape(2, 2, length // LANES, zl, EDGE, LANES)

    rows = yl + 2 * EDGE
    copies, waits = [], []
    ring = ((0, 2), (0, 2), (0, r), (0, r), (0, length))
    for side, (z_dst, src, dst) in enumerate(((0, 0, r), (depth + near, zl - near, depth))):
        n_before = len(copies)
        copies.append((3 + side, (), ring, CORNERS, (side,), ring))
        copies += [
            (5 + side, (f,), full(0, r, 0, yl), f, (), full(z_dst, r, EDGE, yl))
            for f in (LEV, IMG)
        ]
        n_halo = len(copies)
        copies.append((7, (), full(src, near, 0, yl), HEA, (), full(dst, near, EDGE, yl)))
        for f in (LEV, IMG):
            copies.append((f, (), full(src, near, 0, yl), f, (), full(dst, near, EDGE, yl)))
            copies += [
                (
                    2, (t, f, lane // LANES), ((src, near), (0, EDGE), (0, LANES)),
                    f, (), ((dst, near), (row, EDGE), (lane, LANES)),
                )
                for t, row in ((0, 0), (1, EDGE + yl))
                for lane in range(0, length, LANES)
            ]
        waits.append((tuple(range(n_before, n_halo)), tuple(range(n_halo, len(copies)))))
    whole = ((0, rows, True),)
    inside = ((0, EDGE, True), (EDGE, yl, False), (EDGE + yl, EDGE, True))
    side_steps = EDGE // PAIR
    z_edges = dict(
        name="z_edges", rows=rows, rows_out=yl, length=length, planes=2 * depth,
        pair=PAIR, steps=2 * side_steps,
        base=lambda t: depth * (t // side_steps) + PAIR * (t % side_steps),
        out_z=lambda t: (zl - EDGE) * (t // side_steps) + PAIR * (t % side_steps),
        groups=((EDGE, yl, 0),), local_at=(LEV, IMG),
        copies=copies,
        first=waits[0][0] + waits[0][1],
        fills=[
            (waits[0][0], (), 0, (0, r), whole),
            (waits[0][1], waits[1][0] + waits[1][1], None, (r, depth), inside),
        ],
        late_fills=(
            side_steps // 2 - 1,
            [
                (waits[1][0], (), 1, (depth + near, 2 * depth), whole),
                (waits[1][1], (), None, (depth, depth + near), inside),
            ],
        ),
        corners=(0, depth + near),
        h_export=(), z_export=(), late_waits=(), extra_out=[],
    )
    (out,) = run_part(
        z_edges, shape,
        [level_set, image, y_strips, corner_before, corner_after, z_before, z_after, hea],
        doubled(y_rows, np.arange(-EDGE, yl + EDGE)), wx, out,
    )
    return out


def solution(mesh):
    return jax.shard_map(
        body,
        mesh=mesh,
        in_specs=(P("col", "row", None), P("col", "row", None)),
        out_specs=P("col", "row", None),
        check_vma=False,
    )
```

```python
import functools
import math

import jax
import jax.numpy as jnp
import numpy as np
from jax import lax
from jax.experimental import pallas as pl
from jax.experimental.pallas import tpu as pltpu
from jax.sharding import PartitionSpec as P

RADIUS = 6
PAIR = 2
EDGE = 8
TILE = 16
LANES = 128

sigma_cells = 8.0
dt_step = 0.5
nu_diff = 0.1
eps_fit = 0.05

ATAN_COEFS = (
    0.318309854, -0.106098923, 0.0635640505, -0.0446161759,
    0.0315320858, -0.0188971351, 0.00769233704, -0.0014861167,
)
TAP_SCALE = 0.519


def taps():
    d = np.arange(RADIUS + 1, dtype=np.float64)
    exact = np.exp(-d * d / (2.0 * sigma_cells * sigma_cells))
    short = np.asarray((TAP_SCALE * exact).astype(np.float32).astype(jnp.bfloat16))
    short64 = short.astype(np.float64)
    short_sum = short64[0] + 2.0 * short64[1:].sum()
    z_taps = exact / (exact[0] + 2.0 * exact[1:].sum()) / (short_sum * short_sum)
    return [float(v) for v in z_taps], short


def band(out_pos, in_pos, period=None):
    _, short = taps()
    dist = np.abs(out_pos[:, None] - in_pos[None, :])
    if period is not None:
        dist = np.minimum(dist, period - dist)
    table = np.where(dist <= RADIUS, short.astype(np.float32)[np.minimum(dist, RADIUS)], 0.0)
    return jnp.asarray(table.astype(np.float32), jnp.bfloat16)


def heaviside(x, scale):
    far = jnp.abs(x) > 1.0
    t = jnp.where(far, pl.reciprocal(x, approx=False), x)
    z = t * t
    p = ATAN_COEFS[-1] * scale
    for c in ATAN_COEFS[-2::-1]:
        p = p * z + c * scale
    p = p * t
    base = jnp.where(far, jnp.where(x > 0.0, scale, 0.0), 0.5 * scale)
    return base + jnp.where(far, -p, p)


def interleave(first, second):
    a, b = len(first), len(second)
    done = 0
    for i, piece in enumerate(first):
        piece()
        want = (i + 1) * b // a
        while done < want:
            second[done]()
            done += 1


def split_bf16(acc):
    hi = acc.astype(jnp.bfloat16)
    return hi, (acc - hi.astype(jnp.float32)).astype(jnp.bfloat16)


def part_kernel(plan, *refs):
    srcs, (wy_ref,), wx_ref, _, outs, scratch = plan["unpack"](refs)
    out_ref = outs[0]
    lev, img, hea, him, sqr, zb0, zb1, xb, xr, ob, in_sem, out_sem, exp_sem = scratch[:13]
    rows, rows_out, length = plan["rows"], plan["rows_out"], plan["length"]
    groups, steps, pair = plan["groups"], plan["steps"], plan["pair"]
    z_taps, _ = taps()
    sim = scratch[-1]
    fields = (him, hea, sim, sqr)

    def copy_in(k):
        src, lead, src_ranges, dst, dst_lead, dst_ranges = plan["copies"][k]
        src, dst = srcs[src], scratch[dst]
        for i in lead:
            src = src.at[i]
        for i in dst_lead:
            dst = dst.at[i]
        return pltpu.make_async_copy(
            src.at[tuple(pl.ds(a, n) for a, n in src_ranges)],
            dst.at[tuple(pl.ds(a, n) for a, n in dst_ranges)],
            in_sem.at[k],
        )

    for k in plan["first"]:
        copy_in(k).start()

    def ready_copy(t):
        part = pl.ds(pair * t, pair)
        return pltpu.make_async_copy(
            srcs[plan["ready_src"]].at[part], scratch[READY].at[part], scratch[READY_SEM].at[t]
        )

    def transpose_strips():
        held, strip = scratch[16], scratch[17]
        for k in plan["strip_waits"]:
            copy_in(k).wait()
        for k in plan["late_waits"]:
            copy_in(k).start()

        def start_ready(t, carry):
            ready_copy(t).start()
            return carry

        lax.fori_loop(0, steps, start_ready, 0)
        n_z = held.shape[3]

        def block(b, carry):
            z0 = pl.multiple_of(b * 8, 8)
            for side in range(2):
                for f in range(2):
                    for row in range(EDGE):
                        y = max(row - (EDGE - RADIUS), 0) if side == 0 else min(row, RADIUS - 1)
                        for lane in range(0, length, LANES):
                            strip[
                                side, f, lane // LANES, pl.ds(z0 * EDGE + row, 8, stride=EDGE), :
                            ] = held[side, f, y, pl.ds(z0, 8), pl.ds(lane, LANES)]
            return carry

        lax.fori_loop(0, n_z // 8, block, 0)
        copy = pltpu.make_async_copy(strip, outs[1], exp_sem.at[0])
        copy.start()

        def spread(z, carry):
            rows8 = pl.ds(pl.multiple_of(z * EDGE, EDGE), EDGE)
            for side in range(2):
                for f, (halo, near) in enumerate(((lev, scratch[14]), (img, scratch[15]))):
                    at = side * (near.shape[1] - EDGE)
                    for lane in range(0, length, LANES):
                        v = strip[side, f, lane // LANES, rows8, :]
                        halo[z, side * EDGE : (side + 1) * EDGE, lane : lane + LANES] = v
                        near[z, at : at + EDGE, lane : lane + LANES] = v
            return carry

        lax.fori_loop(0, n_z, spread, 0)
        return copy

    strip_copy = transpose_strips() if plan["strip_waits"] else None

    def fill(z, carry, spans):
        for a, n, compute in spans:
            for at in range(a, a + n, 8):
                for lane in range(0, length, LANES):
                    where = (z, pl.ds(at, 8), pl.ds(lane, LANES))
                    if compute:
                        h = heaviside(lev[where], z_taps[0])
                        hea[where] = h
                    else:
                        h = hea[where]
                    im = img[where]
                    him[where] = h * im
                    scaled = im * z_taps[0]
                    sim[where] = scaled
                    sqr[where] = scaled * im
        return carry

    def place_corners(side):
        held = scratch[13]
        z0 = plan["corners"][side]
        for t, row, pad in ((0, EDGE - RADIUS, 0), (1, rows - EDGE, rows - EDGE + RADIUS)):
            for f, dst in enumerate((lev, img)):
                for z in range(RADIUS):
                    dst[z0 + z, row : row + RADIUS, :] = held[side, t, f, z]
                    dst[z0 + z, pad : pad + EDGE - RADIUS, :] = jnp.zeros(
                        (EDGE - RADIUS, length), jnp.float32
                    )

    def run_fills(fills):
        for waits, starts, corner_side, (z0, z1), spans in fills:
            for k in waits:
                copy_in(k).wait()
            for k in starts:
                copy_in(k).start()
            if corner_side is not None:
                place_corners(corner_side)
            lax.fori_loop(z0, z1, functools.partial(fill, spans=spans), 0)

    run_fills(plan["fills"])

    exports = []
    for e, (a, n) in enumerate(plan["h_export"]):
        copy = pltpu.make_async_copy(
            hea.at[pl.ds(a, n)], outs[1].at[pl.ds(a, n)], exp_sem.at[e]
        )
        copy.start()
        exports.append(copy)

    def z_tile(first, zb, at, col):
        def emit():
            sums = []
            for tile in (col, col + LANES):
                f, lane = divmod(tile, length)
                vals = [
                    fields[f][first + z, pl.ds(at, TILE), pl.ds(lane, LANES)]
                    for z in range(pair + 2 * RADIUS)
                ]
                for z in range(pair):
                    acc = vals[z + RADIUS]
                    for d in range(1, RADIUS + 1):
                        acc = acc + (vals[z + RADIUS - d] + vals[z + RADIUS + d]) * (
                            z_taps[d] / z_taps[0]
                        )
                    sums.append(acc)
            for z in range(pair):
                hi, lo = split_bf16(jnp.concatenate([sums[z], sums[pair + z]], axis=1))
                zb[z, pl.ds(at, TILE), pl.ds(col, wide)] = hi
                zb[z, pl.ds(at + rows, TILE), pl.ds(col, wide)] = lo

        return emit

    def z_pieces(first, zb, row_starts):
        return [
            z_tile(first, zb, at, col) for at in row_starts for col in range(0, 4 * length, wide)
        ]

    wide = 2 * LANES

    def along_y(t, z, zb, col):
        def emit():
            values = zb[z, :, col : col + wide]
            if plan["ready"]:
                near = scratch[READY][pair * t + z, :, col : col + wide]
                values = jnp.concatenate([values, near], axis=0)
            acc = jnp.dot(wy_ref[...], values, preferred_element_type=jnp.float32)
            whole = col // length == (col + wide - 1) // length
            step = wide if whole else LANES
            for part in range(0, wide, step):
                hi, lo = split_bf16(acc[:, part : part + step])
                f, x = divmod(col + part, length)
                at = (z * 4 + f) * rows_out
                xb[at : at + rows_out, x : x + step] = hi
                xb[at : at + rows_out, length + x : length + x + step] = lo

        return emit

    def along_x(z, planes):
        def emit():
            at, n = z * 4 * rows_out, planes * 4 * rows_out
            xr[at : at + n, :] = jnp.dot(
                xb[at : at + n, :], wx_ref[...], preferred_element_type=jnp.float32
            )

        return emit

    def update(t, z, zi, row, at):
        def emit():
            for lane in range(0, length, LANES):
                s1, s2, s3, s4 = (
                    xr[
                        (z * 4 + f) * rows_out + row : (z * 4 + f) * rows_out + row + 8,
                        lane : lane + LANES,
                    ]
                    for f in range(4)
                )
                lv, im, others = local_of(*plan["local_at"])(scratch, zi, at, lane, length)
                inner = s2 + eps_fit
                outer = (1.0 + eps_fit) - s2
                spread = s4 - (s3 * s3 - eps_fit)
                left = s1 * outer
                right = (s3 - s1) * inner
                prod = inner * outer
                pi_dt = math.pi / dt_step
                denom = (prod * prod) * (spread * (pi_dt + (pi_dt * lv) * lv))
                numer = (left - right) * ((im + im) * prod - (left + right))
                ob[pair * t + z, row : row + 8, lane : lane + LANES] = (
                    (1.0 - 6.0 * dt_step * nu_diff) * lv
                    + (dt_step * nu_diff) * others
                    + numer * pl.reciprocal(denom, approx=False)
                )

        return emit

    def yxf_pieces(t, zb):
        zi = plan["base"](t) + RADIUS
        pieces = [
            along_y(t, z, zb, col) for z in range(pair) for col in range(0, 4 * length, wide)
        ]
        together = pair if pair * rows_out <= 64 else 1
        pieces += [along_x(z, together) for z in range(0, pair, together)]
        for z in range(pair):
            row = 0
            for start, count, _ in groups:
                pieces += [update(t, z, zi + z, row + i, start + i) for i in range(0, count, 8)]
                row += count
        return pieces

    def out_copies(t):
        row, made = 0, []
        for g, (_, count, y0) in enumerate(groups):
            made.append(
                pltpu.make_async_copy(
                    ob.at[pl.ds(pair * t, pair), pl.ds(row, count), :],
                    out_ref.at[pl.ds(plan["out_z"](t), pair), pl.ds(y0, count), :],
                    out_sem.at[t, g],
                )
            )
            row += count
        return made

    n_h = len(plan["h_export"])

    def z_export(t, zb, slot):
        return [
            pltpu.make_async_copy(
                zb.at[:, pl.ds(src, TILE), :],
                outs[2].at[pl.ds(pair * t, pair), pl.ds(TILE * e, TILE), :],
                exp_sem.at[n_h + len(plan["z_export"]) * slot + e],
            )
            for e, src in enumerate(plan["z_export"])
        ]

    def prologue(r, carry):
        at = pl.multiple_of(r * TILE, TILE)
        for piece in z_pieces(plan["base"](0), zb0, [at]):
            piece()
        return carry

    lax.fori_loop(0, rows // TILE, prologue, 0)
    for copy in z_export(0, zb0, 0):
        copy.start()
    for k in plan["late_waits"]:
        copy_in(k).wait()
    tiles = list(range(0, rows, TILE))

    n_pairs = steps // 2

    def two_steps(i, last):
        for half, (now, nxt) in enumerate(((zb0, zb1), (zb1, zb0))):
            t = 2 * i + half
            if plan["ready"]:
                ready_copy(t).wait()
            ahead = half == 0 or not last
            if plan["z_export"] and ahead:
                if half == 1:
                    for copy in z_export(t - 1, nxt, 0):
                        copy.wait()
                elif last:
                    for copy in z_export(t - 1, nxt, 1):
                        copy.wait()
                else:

                    @pl.when(i > 0)
                    def _():
                        for copy in z_export(t - 1, nxt, 1):
                            copy.wait()

            z_work = z_pieces(plan["base"](t + 1), nxt, tiles) if ahead else []
            interleave(yxf_pieces(t, now), z_work)
            for copy in out_copies(t):
                copy.start()
            if plan["z_export"] and ahead:
                for copy in z_export(t + 1, nxt, 1 - half):
                    copy.start()

    def steady(i, carry):
        if plan["late_fills"]:
            at, fills = plan["late_fills"]
            pl.when(i == at)(lambda: run_fills(fills))
        two_steps(i, False)
        return carry

    lax.fori_loop(0, n_pairs - 1, steady, 0)
    two_steps(n_pairs - 1, True)
    if plan["z_export"]:
        for slot, zb in ((0, zb0), (1, zb1)):
            for copy in z_export(steps - 2 + slot, zb, slot):
                copy.wait()
    for copy in exports + ([] if strip_copy is None else [strip_copy]):
        copy.wait()

    def finish(t, carry):
        for copy in out_copies(t):
            copy.wait()
        return carry

    lax.fori_loop(0, steps, finish, 0)


def run_part(plan, shape, srcs, wy, wx, prev):
    rows, rows_out, length, planes = plan["rows"], plan["rows_out"], plan["length"], plan["planes"]
    steps, pair, n_ready = plan["steps"], plan["pair"], plan.get("ready", 0)
    n_src, n_wy, n_out = len(srcs), 1, 1 + len(plan["extra_out"])
    n_prev = 0 if prev is None else 1

    def unpack(refs):
        cuts = np.cumsum([n_src, n_wy, 1, n_prev, n_out])
        a, b, c, d, e = (int(v) for v in cuts)
        return refs[:a], refs[a:b], refs[b], refs[c:d], refs[d:e], refs[e:]

    plan = dict(plan, unpack=unpack, ready=n_ready, strip_waits=plan.get("strip_waits", ()),
        late_fills=plan.get("late_fills"))
    any_spec = pl.BlockSpec(memory_space=pl.ANY)
    vmem = pl.BlockSpec(memory_space=pltpu.VMEM)
    args = list(srcs) + [wy, wx] + ([] if prev is None else [prev])
    specs = [any_spec] * n_src + [vmem] * (n_wy + 1) + [any_spec] * n_prev
    n_elem = pair * steps * rows_out * length
    field = pltpu.VMEM((planes, rows, length), jnp.float32)
    taps_buffer = pltpu.VMEM((pair, 2 * rows, 4 * length), jnp.bfloat16)
    scratch = [field] * 5 + [
        taps_buffer,
        taps_buffer,
        pltpu.VMEM((pair * 4 * rows_out, 2 * length), jnp.bfloat16),
        pltpu.VMEM((pair * 4 * rows_out, length), jnp.float32),
        pltpu.VMEM((pair * steps, rows_out, length), jnp.float32),
        pltpu.SemaphoreType.DMA((len(plan["copies"]),)),
        pltpu.SemaphoreType.DMA((steps, len(plan["groups"]))),
        pltpu.SemaphoreType.DMA((max(1, len(plan["h_export"]) + 2 * len(plan["z_export"])),)),
    ]
    if n_ready:
        scratch += [
            pltpu.VMEM((pair * steps, n_ready, 4 * length), jnp.bfloat16),
            pltpu.VMEM((planes, 2 * (EDGE + TILE), length), jnp.float32),
            pltpu.VMEM((planes, 2 * (EDGE + TILE), length), jnp.float32),
            pltpu.VMEM((2, 2, RADIUS, planes, length), jnp.float32),
            pltpu.VMEM((2, 2, length // LANES, planes * EDGE, LANES), jnp.float32),
            pltpu.SemaphoreType.DMA((steps,)),
        ]
    if plan.get("corners"):
        scratch.append(pltpu.VMEM((2, 2, 2, RADIUS, RADIUS, length), jnp.float32))
    scratch.append(field)
    out = pl.pallas_call(
        functools.partial(part_kernel, plan),
        out_shape=[jax.ShapeDtypeStruct(shape, jnp.float32)] + plan["extra_out"],
        in_specs=specs,
        out_specs=[any_spec] * n_out,
        scratch_shapes=scratch,
        input_output_aliases={} if prev is None else {len(args) - 1: 0},
        compiler_params=pltpu.CompilerParams(
            vmem_limit_bytes=60 * 1024 * 1024,
        ),
        cost_estimate=pl.CostEstimate(
            flops=n_elem * 12000, bytes_accessed=n_elem * 12, transcendentals=0
        ),
        name=plan["name"],
    )(*args)
    return out


def neighbours(axis):
    n = lax.axis_size(axis)
    up = [(i, (i + 1) % n) for i in range(n)]
    return up, [(j, i) for i, j in up]


def local_of(lev_at, img_at):
    def local(scratch, zi, at, lane, length):
        lev, img = scratch[lev_at], scratch[img_at]
        cols = slice(lane, lane + LANES)
        lv = lev[zi, at : at + 8, cols]
        last = LANES - 1
        prev = lev[zi, at : at + 8, (lane - LANES) % length : (lane - LANES) % length + LANES]
        follow = lev[zi, at : at + 8, (lane + LANES) % length : (lane + LANES) % length + LANES]
        index = lax.broadcasted_iota(jnp.int32, (8, LANES), 1)
        here_up, here_down = pltpu.roll(lv, 1, 1), pltpu.roll(lv, last, 1)
        west = jnp.where(index == 0, pltpu.roll(prev, 1, 1), here_up)
        east = jnp.where(index == last, pltpu.roll(follow, last, 1), here_down)
        others = (
            (lev[zi - 1, at : at + 8, cols] + lev[zi + 1, at : at + 8, cols])
            + (lev[zi, at - 1 : at + 7, cols] + lev[zi, at + 1 : at + 9, cols])
            + (west + east)
        )
        return lv, img[zi, at : at + 8, cols], others

    return local


LEV, IMG, HEA, READY, NEAR_LEV, NEAR_IMG, HELD = 0, 1, 2, 13, 14, 15, 16
CORNERS, READY_SEM = 13, 18


def body(level_set, image):
    zl, yl, length = level_set.shape
    shape = level_set.shape
    r = RADIUS
    both = jnp.stack([level_set, image])
    y_up, y_down = neighbours("row")
    z_up, z_down = neighbours("col")

    y_before = lax.ppermute(both[:, :, yl - r :, :].transpose(0, 2, 1, 3), "row", y_up)
    y_after = lax.ppermute(both[:, :, :r, :].transpose(0, 2, 1, 3), "row", y_down)
    z_before = lax.ppermute(both[:, zl - r :], "col", z_up)
    z_after = lax.ppermute(both[:, :r], "col", z_down)

    y_rows = np.arange(yl)
    wx1 = band(np.arange(length), np.arange(length), length)
    wx = jnp.concatenate([wx1, wx1], axis=0)

    def doubled(out_pos, in_pos):
        w = band(out_pos, in_pos)
        return jnp.concatenate([w, w], axis=1)

    def full(z0, zn, y0, yn):
        return ((z0, zn), (y0, yn), (0, length))

    depth = PAIR * 4 + 2 * r
    near = depth - r
    inner = zl - 2 * EDGE
    chunk = zl // 6 if zl % 6 == 0 else zl // 3
    n_chunks = zl // chunk
    interior = dict(
        name="interior", rows=yl, rows_out=yl - 2 * EDGE, length=length, planes=zl,
        pair=PAIR, steps=inner // PAIR,
        base=lambda t: EDGE - r + PAIR * t, out_z=lambda t: EDGE + PAIR * t,
        groups=((EDGE, yl - 2 * EDGE, EDGE),), local_at=(LEV, IMG),
        copies=[
            (f, (), full(z, chunk, 0, yl), f, (), full(z, chunk, 0, yl))
            for z in range(0, zl, chunk) for f in (LEV, IMG)
        ],
        fills=[
            (
                (2 * c, 2 * c + 1),
                (2 * c + 4, 2 * c + 5) if c + 2 < n_chunks else (),
                None, (c * chunk, (c + 1) * chunk), ((0, yl, True),),
            )
            for c in range(n_chunks)
        ],
        first=range(4),
        h_export=((0, near), (zl - near, near)),
        z_export=(0, yl - TILE, yl, 2 * yl - TILE),
        late_waits=(),
        extra_out=[
            jax.ShapeDtypeStruct(shape, jnp.float32),
            jax.ShapeDtypeStruct((inner, 4 * TILE, 4 * length), jnp.bfloat16),
        ],
    )
    out, hea, near_rows = run_part(
        interior, shape, [level_set, image],
        doubled(y_rows[EDGE : yl - EDGE], y_rows), wx, None,
    )

    edge_last = jnp.stack([y_before[:, :, zl - r :], y_after[:, :, zl - r :]])
    edge_first = jnp.stack([y_before[:, :, :r], y_after[:, :, :r]])
    corner_before = lax.ppermute(edge_last.transpose(0, 1, 3, 2, 4), "col", z_up)
    corner_after = lax.ppermute(edge_first.transpose(0, 1, 3, 2, 4), "col", z_down)

    half = EDGE + TILE
    z_lo, z_n = EDGE - r, zl - 2 * (EDGE - r)
    halo = ((0, r), (0, zl), (0, length))
    copies = [(2 + side, (f,), halo, HELD, (side, f), halo) for side in range(2) for f in range(2)]
    n_first = len(copies)
    for f, dst in ((0, NEAR_LEV), (1, NEAR_IMG)):
        copies += [
            (f, (), full(z_lo, z_n, 0, TILE), dst, (), full(z_lo, z_n, EDGE, TILE)),
            (f, (), full(z_lo, z_n, yl - TILE, TILE), dst, (), full(z_lo, z_n, half, TILE)),
        ]
    y_edges = dict(
        name="y_edges", rows=2 * EDGE, rows_out=2 * EDGE, length=length, planes=zl,
        pair=2 * PAIR, steps=inner // (2 * PAIR),
        base=lambda t: EDGE - r + 2 * PAIR * t, out_z=lambda t: EDGE + 2 * PAIR * t,
        first=range(n_first),
        groups=((EDGE, EDGE, 0), (half + EDGE, EDGE, yl - EDGE)),
        local_at=(NEAR_LEV, NEAR_IMG),
        copies=copies,
        fills=[((), (), None, (z_lo, z_lo + z_n), ((0, 2 * EDGE, True),))],
        h_export=(), z_export=(), late_waits=tuple(range(n_first, len(copies))),
        extra_out=[
            jax.ShapeDtypeStruct((2, 2, length // LANES, zl * EDGE, LANES), jnp.float32)
        ],
        ready=4 * TILE, ready_src=4, strip_waits=tuple(range(n_first)),
    )
    out_pos = np.concatenate([y_rows[:EDGE], y_rows[yl - EDGE :]])
    halo_pos = np.concatenate([np.arange(-EDGE, 0), np.arange(yl, yl + EDGE)])
    near_pos = np.concatenate([np.arange(TILE), np.arange(yl - TILE, yl)])
    out, y_strips = run_part(
        y_edges, shape, [level_set, image, y_before, y_after, near_rows],
        jnp.concatenate([doubled(out_pos, halo_pos), doubled(out_pos, near_pos)], axis=1),
        wx, out,
    )
    y_strips = y_strips.reshape(2, 2, length // LANES, zl, EDGE, LANES)

    rows = yl + 2 * EDGE
    copies, waits = [], []
    ring = ((0, 2), (0, 2), (0, r), (0, r), (0, length))
    for side, (z_dst, src, dst) in enumerate(((0, 0, r), (depth + near, zl - near, depth))):
        n_before = len(copies)
        copies.append((3 + side, (), ring, CORNERS, (side,), ring))
        copies += [
            (5 + side, (f,), full(0, r, 0, yl), f, (), full(z_dst, r, EDGE, yl))
            for f in (LEV, IMG)
        ]
        n_halo = len(copies)
        copies.append((7, (), full(src, near, 0, yl), HEA, (), full(dst, near, EDGE, yl)))
        for f in (LEV, IMG):
            copies.append((f, (), full(src, near, 0, yl), f, (), full(dst, near, EDGE, yl)))
            copies += [
                (
                    2, (t, f, lane // LANES), ((src, near), (0, EDGE), (0, LANES)),
                    f, (), ((dst, near), (row, EDGE), (lane, LANES)),
                )
                for t, row in ((0, 0), (1, EDGE + yl))
                for lane in range(0, length, LANES)
            ]
        waits.append((tuple(range(n_before, n_halo)), tuple(range(n_halo, len(copies)))))
    whole = ((0, rows, True),)
    inside = ((0, EDGE, True), (EDGE, yl, False), (EDGE + yl, EDGE, True))
    side_steps = EDGE // PAIR
    z_edges = dict(
        name="z_edges", rows=rows, rows_out=yl, length=length, planes=2 * depth,
        pair=PAIR, steps=2 * side_steps,
        base=lambda t: depth * (t // side_steps) + PAIR * (t % side_steps),
        out_z=lambda t: (zl - EDGE) * (t // side_steps) + PAIR * (t % side_steps),
        groups=((EDGE, yl, 0),), local_at=(LEV, IMG),
        copies=copies,
        first=waits[0][0] + waits[0][1],
        fills=[
            (waits[0][0], (), 0, (0, r), whole),
            (waits[0][1], waits[1][0] + waits[1][1], None, (r, depth), inside),
        ],
        late_fills=(
            side_steps // 2 - 1,
            [
                (waits[1][0], (), 1, (depth + near, 2 * depth), whole),
                (waits[1][1], (), None, (depth, depth + near), inside),
            ],
        ),
        corners=(0, depth + near),
        h_export=(), z_export=(), late_waits=(), extra_out=[],
    )
    (out,) = run_part(
        z_edges, shape,
        [level_set, image, y_strips, corner_before, corner_after, z_before, z_after, hea],
        doubled(y_rows, np.arange(-EDGE, yl + EDGE)), wx, out,
    )
    return out


def solution(mesh):
    return jax.shard_map(
        body,
        mesh=mesh,
        in_specs=(P("col", "row", None), P("col", "row", None)),
        out_specs=P("col", "row", None),
        check_vma=False,
    )
```

```python
import functools
import math

import jax
import jax.numpy as jnp
import numpy as np
from jax import lax
from jax.experimental import pallas as pl
from jax.experimental.pallas import tpu as pltpu
from jax.sharding import PartitionSpec as P

RADIUS = 6
PAIR = 2
EDGE = 8
TILE = 16
LANES = 128

sigma_cells = 8.0
dt_step = 0.5
nu_diff = 0.1
eps_fit = 0.05

ATAN_COEFS = (
    0.318309854, -0.106098923, 0.0635640505, -0.0446161759,
    0.0315320858, -0.0188971351, 0.00769233704, -0.0014861167,
)
TAP_SCALE = 0.519


def taps():
    d = np.arange(RADIUS + 1, dtype=np.float64)
    exact = np.exp(-d * d / (2.0 * sigma_cells * sigma_cells))
    short = np.asarray((TAP_SCALE * exact).astype(np.float32).astype(jnp.bfloat16))
    short64 = short.astype(np.float64)
    short_sum = short64[0] + 2.0 * short64[1:].sum()
    z_taps = exact / (exact[0] + 2.0 * exact[1:].sum()) / (short_sum * short_sum)
    return [float(v) for v in z_taps], short


def band(out_pos, in_pos, period=None):
    _, short = taps()
    dist = np.abs(out_pos[:, None] - in_pos[None, :])
    if period is not None:
        dist = np.minimum(dist, period - dist)
    table = np.where(dist <= RADIUS, short.astype(np.float32)[np.minimum(dist, RADIUS)], 0.0)
    return jnp.asarray(table.astype(np.float32), jnp.bfloat16)


def heaviside(x, scale):
    far = jnp.abs(x) > 1.0
    t = jnp.where(far, pl.reciprocal(x, approx=False), x)
    z = t * t
    p = ATAN_COEFS[-1] * scale
    for c in ATAN_COEFS[-2::-1]:
        p = p * z + c * scale
    p = p * t
    base = jnp.where(far, jnp.where(x > 0.0, scale, 0.0), 0.5 * scale)
    return base + jnp.where(far, -p, p)


def interleave(first, second):
    a, b = len(first), len(second)
    done = 0
    for i, piece in enumerate(first):
        piece()
        want = (i + 1) * b // a
        while done < want:
            second[done]()
            done += 1


def split_bf16(acc):
    hi = acc.astype(jnp.bfloat16)
    return hi, (acc - hi.astype(jnp.float32)).astype(jnp.bfloat16)


def part_kernel(plan, *refs):
    srcs, (wy_ref,), wx_ref, _, outs, scratch = plan["unpack"](refs)
    out_ref = outs[0]
    lev, img, hea, him, sqr, zb0, zb1, xb, xr, ob, in_sem, out_sem, exp_sem = scratch[:13]
    rows, rows_out, length = plan["rows"], plan["rows_out"], plan["length"]
    groups, steps, pair = plan["groups"], plan["steps"], plan["pair"]
    z_taps, _ = taps()
    sim = scratch[-1]
    fields = (him, hea, sim, sqr)

    def copy_in(k):
        src, lead, src_ranges, dst, dst_lead, dst_ranges = plan["copies"][k]
        src, dst = srcs[src], scratch[dst]
        for i in lead:
            src = src.at[i]
        for i in dst_lead:
            dst = dst.at[i]
        return pltpu.make_async_copy(
            src.at[tuple(pl.ds(a, n) for a, n in src_ranges)],
            dst.at[tuple(pl.ds(a, n) for a, n in dst_ranges)],
            in_sem.at[k],
        )

    for k in plan["first"]:
        copy_in(k).start()

    def ready_copy(t):
        part = pl.ds(pair * t, pair)
        return pltpu.make_async_copy(
            srcs[plan["ready_src"]].at[part], scratch[READY].at[part], scratch[READY_SEM].at[t]
        )

    def transpose_strips():
        held, strip = scratch[16], scratch[17]
        for k in plan["late_waits"]:
            copy_in(k).start()

        def start_ready(t, carry):
            ready_copy(t).start()
            return carry

        lax.fori_loop(0, steps, start_ready, 0)
        for k in plan["strip_waits"]:
            copy_in(k).wait()
        n_z = held.shape[3]

        def block(b, carry):
            z0 = pl.multiple_of(b * 8, 8)
            for side in range(2):
                for f in range(2):
                    for row in range(EDGE):
                        y = max(row - (EDGE - RADIUS), 0) if side == 0 else min(row, RADIUS - 1)
                        for lane in range(0, length, LANES):
                            strip[
                                side, f, lane // LANES, pl.ds(z0 * EDGE + row, 8, stride=EDGE), :
                            ] = held[side, f, y, pl.ds(z0, 8), pl.ds(lane, LANES)]
            return carry

        lax.fori_loop(0, n_z // 8, block, 0)
        copy = pltpu.make_async_copy(strip, outs[1], exp_sem.at[0])
        copy.start()

        def spread(z, carry):
            rows8 = pl.ds(pl.multiple_of(z * EDGE, EDGE), EDGE)
            for side in range(2):
                for f, (halo, near) in enumerate(((lev, scratch[14]), (img, scratch[15]))):
                    at = side * (near.shape[1] - EDGE)
                    for lane in range(0, length, LANES):
                        v = strip[side, f, lane // LANES, rows8, :]
                        halo[z, side * EDGE : (side + 1) * EDGE, lane : lane + LANES] = v
                        near[z, at : at + EDGE, lane : lane + LANES] = v
            return carry

        lax.fori_loop(0, n_z, spread, 0)
        return copy

    strip_copy = transpose_strips() if plan["strip_waits"] else None

    def fill(z, carry, spans):
        for a, n, compute in spans:
            for at in range(a, a + n, 8):
                for lane in range(0, length, LANES):
                    where = (z, pl.ds(at, 8), pl.ds(lane, LANES))
                    if compute:
                        h = heaviside(lev[where], z_taps[0])
                        hea[where] = h
                    else:
                        h = hea[where]
                    im = img[where]
                    him[where] = h * im
                    scaled = im * z_taps[0]
                    sim[where] = scaled
                    sqr[where] = scaled * im
        return carry

    def place_corners(side):
        held = scratch[13]
        z0 = plan["corners"][side]
        for t, row, pad in ((0, EDGE - RADIUS, 0), (1, rows - EDGE, rows - EDGE + RADIUS)):
            for f, dst in enumerate((lev, img)):
                for z in range(RADIUS):
                    dst[z0 + z, row : row + RADIUS, :] = held[side, t, f, z]
                    dst[z0 + z, pad : pad + EDGE - RADIUS, :] = jnp.zeros(
                        (EDGE - RADIUS, length), jnp.float32
                    )

    def run_fills(fills):
        for waits, starts, corner_side, (z0, z1), spans in fills:
            for k in waits:
                copy_in(k).wait()
            for k in starts:
                copy_in(k).start()
            if corner_side is not None:
                place_corners(corner_side)
            lax.fori_loop(z0, z1, functools.partial(fill, spans=spans), 0)

    run_fills(plan["fills"])

    exports = []
    for e, (a, n) in enumerate(plan["h_export"]):
        copy = pltpu.make_async_copy(
            hea.at[pl.ds(a, n)], outs[1].at[pl.ds(a, n)], exp_sem.at[e]
        )
        copy.start()
        exports.append(copy)

    def z_tile(first, zb, at, col):
        def emit():
            sums = []
            for tile in (col, col + LANES):
                f, lane = divmod(tile, length)
                vals = [
                    fields[f][first + z, pl.ds(at, TILE), pl.ds(lane, LANES)]
                    for z in range(pair + 2 * RADIUS)
                ]
                for z in range(pair):
                    acc = vals[z + RADIUS]
                    for d in range(1, RADIUS + 1):
                        acc = acc + (vals[z + RADIUS - d] + vals[z + RADIUS + d]) * (
                            z_taps[d] / z_taps[0]
                        )
                    sums.append(acc)
            for z in range(pair):
                hi, lo = split_bf16(jnp.concatenate([sums[z], sums[pair + z]], axis=1))
                zb[z, pl.ds(at, TILE), pl.ds(col, wide)] = hi
                zb[z, pl.ds(at + rows, TILE), pl.ds(col, wide)] = lo

        return emit

    def z_pieces(first, zb, row_starts):
        return [
            z_tile(first, zb, at, col) for at in row_starts for col in range(0, 4 * length, wide)
        ]

    wide = 2 * LANES

    def along_y(t, z, zb, col):
        def emit():
            values = zb[z, :, col : col + wide]
            if plan["ready"]:
                near = scratch[READY][pair * t + z, :, col : col + wide]
                values = jnp.concatenate([values, near], axis=0)
            acc = jnp.dot(wy_ref[...], values, preferred_element_type=jnp.float32)
            whole = col // length == (col + wide - 1) // length
            step = wide if whole else LANES
            for part in range(0, wide, step):
                hi, lo = split_bf16(acc[:, part : part + step])
                f, x = divmod(col + part, length)
                at = (z * 4 + f) * rows_out
                xb[at : at + rows_out, x : x + step] = hi
                xb[at : at + rows_out, length + x : length + x + step] = lo

        return emit

    def along_x(z, planes):
        def emit():
            at, n = z * 4 * rows_out, planes * 4 * rows_out
            xr[at : at + n, :] = jnp.dot(
                xb[at : at + n, :], wx_ref[...], preferred_element_type=jnp.float32
            )

        return emit

    def update(t, z, zi, row, at):
        def emit():
            for lane in range(0, length, LANES):
                s1, s2, s3, s4 = (
                    xr[
                        (z * 4 + f) * rows_out + row : (z * 4 + f) * rows_out + row + 8,
                        lane : lane + LANES,
                    ]
                    for f in range(4)
                )
                lv, im, others = local_of(*plan["local_at"])(scratch, zi, at, lane, length)
                inner = s2 + eps_fit
                outer = (1.0 + eps_fit) - s2
                spread = s4 - (s3 * s3 - eps_fit)
                left = s1 * outer
                right = (s3 - s1) * inner
                prod = inner * outer
                pi_dt = math.pi / dt_step
                denom = (prod * prod) * (spread * (pi_dt + (pi_dt * lv) * lv))
                numer = (left - right) * ((im + im) * prod - (left + right))
                ob[pair * t + z, row : row + 8, lane : lane + LANES] = (
                    (1.0 - 6.0 * dt_step * nu_diff) * lv
                    + (dt_step * nu_diff) * others
                    + numer * pl.reciprocal(denom, approx=False)
                )

        return emit

    def yxf_pieces(t, zb):
        zi = plan["base"](t) + RADIUS
        pieces = [
            along_y(t, z, zb, col) for z in range(pair) for col in range(0, 4 * length, wide)
        ]
        together = pair if pair * rows_out <= 64 else 1
        pieces += [along_x(z, together) for z in range(0, pair, together)]
        for z in range(pair):
            row = 0
            for start, count, _ in groups:
                pieces += [update(t, z, zi + z, row + i, start + i) for i in range(0, count, 8)]
                row += count
        return pieces

    def out_copies(t):
        row, made = 0, []
        for g, (_, count, y0) in enumerate(groups):
            made.append(
                pltpu.make_async_copy(
                    ob.at[pl.ds(pair * t, pair), pl.ds(row, count), :],
                    out_ref.at[pl.ds(plan["out_z"](t), pair), pl.ds(y0, count), :],
                    out_sem.at[t, g],
                )
            )
            row += count
        return made

    n_h = len(plan["h_export"])

    def z_export(t, zb, slot):
        return [
            pltpu.make_async_copy(
                zb.at[:, pl.ds(src, TILE), :],
                outs[2].at[pl.ds(pair * t, pair), pl.ds(TILE * e, TILE), :],
                exp_sem.at[n_h + len(plan["z_export"]) * slot + e],
            )
            for e, src in enumerate(plan["z_export"])
        ]

    def prologue(r, carry):
        at = pl.multiple_of(r * TILE, TILE)
        for piece in z_pieces(plan["base"](0), zb0, [at]):
            piece()
        return carry

    lax.fori_loop(0, rows // TILE, prologue, 0)
    for copy in z_export(0, zb0, 0):
        copy.start()
    for k in plan["late_waits"]:
        copy_in(k).wait()
    tiles = list(range(0, rows, TILE))

    n_pairs = steps // 2

    def two_steps(i, last):
        for half, (now, nxt) in enumerate(((zb0, zb1), (zb1, zb0))):
            t = 2 * i + half
            if plan["ready"]:
                ready_copy(t).wait()
            ahead = half == 0 or not last
            if plan["z_export"] and ahead:
                if half == 1:
                    for copy in z_export(t - 1, nxt, 0):
                        copy.wait()
                elif last:
                    for copy in z_export(t - 1, nxt, 1):
                        copy.wait()
                else:

                    @pl.when(i > 0)
                    def _():
                        for copy in z_export(t - 1, nxt, 1):
                            copy.wait()

            z_work = z_pieces(plan["base"](t + 1), nxt, tiles) if ahead else []
            interleave(yxf_pieces(t, now), z_work)
            for copy in out_copies(t):
                copy.start()
            if plan["z_export"] and ahead:
                for copy in z_export(t + 1, nxt, 1 - half):
                    copy.start()

    def steady(i, carry):
        if plan["late_fills"]:
            at, fills = plan["late_fills"]
            pl.when(i == at)(lambda: run_fills(fills))
        two_steps(i, False)
        return carry

    lax.fori_loop(0, n_pairs - 1, steady, 0)
    two_steps(n_pairs - 1, True)
    if plan["z_export"]:
        for slot, zb in ((0, zb0), (1, zb1)):
            for copy in z_export(steps - 2 + slot, zb, slot):
                copy.wait()
    for copy in exports + ([] if strip_copy is None else [strip_copy]):
        copy.wait()

    def finish(t, carry):
        for copy in out_copies(t):
            copy.wait()
        return carry

    lax.fori_loop(0, steps, finish, 0)


def run_part(plan, shape, srcs, wy, wx, prev):
    rows, rows_out, length, planes = plan["rows"], plan["rows_out"], plan["length"], plan["planes"]
    steps, pair, n_ready = plan["steps"], plan["pair"], plan.get("ready", 0)
    n_src, n_wy, n_out = len(srcs), 1, 1 + len(plan["extra_out"])
    n_prev = 0 if prev is None else 1

    def unpack(refs):
        cuts = np.cumsum([n_src, n_wy, 1, n_prev, n_out])
        a, b, c, d, e = (int(v) for v in cuts)
        return refs[:a], refs[a:b], refs[b], refs[c:d], refs[d:e], refs[e:]

    plan = dict(plan, unpack=unpack, ready=n_ready, strip_waits=plan.get("strip_waits", ()),
        late_fills=plan.get("late_fills"))
    any_spec = pl.BlockSpec(memory_space=pl.ANY)
    vmem = pl.BlockSpec(memory_space=pltpu.VMEM)
    args = list(srcs) + [wy, wx] + ([] if prev is None else [prev])
    specs = [any_spec] * n_src + [vmem] * (n_wy + 1) + [any_spec] * n_prev
    n_elem = pair * steps * rows_out * length
    field = pltpu.VMEM((planes, rows, length), jnp.float32)
    taps_buffer = pltpu.VMEM((pair, 2 * rows, 4 * length), jnp.bfloat16)
    scratch = [field] * 5 + [
        taps_buffer,
        taps_buffer,
        pltpu.VMEM((pair * 4 * rows_out, 2 * length), jnp.bfloat16),
        pltpu.VMEM((pair * 4 * rows_out, length), jnp.float32),
        pltpu.VMEM((pair * steps, rows_out, length), jnp.float32),
        pltpu.SemaphoreType.DMA((len(plan["copies"]),)),
        pltpu.SemaphoreType.DMA((steps, len(plan["groups"]))),
        pltpu.SemaphoreType.DMA((max(1, len(plan["h_export"]) + 2 * len(plan["z_export"])),)),
    ]
    if n_ready:
        scratch += [
            pltpu.VMEM((pair * steps, n_ready, 4 * length), jnp.bfloat16),
            pltpu.VMEM((planes, 2 * (EDGE + TILE), length), jnp.float32),
            pltpu.VMEM((planes, 2 * (EDGE + TILE), length), jnp.float32),
            pltpu.VMEM((2, 2, RADIUS, planes, length), jnp.float32),
            pltpu.VMEM((2, 2, length // LANES, planes * EDGE, LANES), jnp.float32),
            pltpu.SemaphoreType.DMA((steps,)),
        ]
    if plan.get("corners"):
        scratch.append(pltpu.VMEM((2, 2, 2, RADIUS, RADIUS, length), jnp.float32))
    scratch.append(field)
    out = pl.pallas_call(
        functools.partial(part_kernel, plan),
        out_shape=[jax.ShapeDtypeStruct(shape, jnp.float32)] + plan["extra_out"],
        in_specs=specs,
        out_specs=[any_spec] * n_out,
        scratch_shapes=scratch,
        input_output_aliases={} if prev is None else {len(args) - 1: 0},
        compiler_params=pltpu.CompilerParams(
            vmem_limit_bytes=60 * 1024 * 1024,
        ),
        cost_estimate=pl.CostEstimate(
            flops=n_elem * 12000, bytes_accessed=n_elem * 12, transcendentals=0
        ),
        name=plan["name"],
    )(*args)
    return out


def neighbours(axis):
    n = lax.axis_size(axis)
    up = [(i, (i + 1) % n) for i in range(n)]
    return up, [(j, i) for i, j in up]


def local_of(lev_at, img_at):
    def local(scratch, zi, at, lane, length):
        lev, img = scratch[lev_at], scratch[img_at]
        cols = slice(lane, lane + LANES)
        lv = lev[zi, at : at + 8, cols]
        last = LANES - 1
        prev = lev[zi, at : at + 8, (lane - LANES) % length : (lane - LANES) % length + LANES]
        follow = lev[zi, at : at + 8, (lane + LANES) % length : (lane + LANES) % length + LANES]
        index = lax.broadcasted_iota(jnp.int32, (8, LANES), 1)
        here_up, here_down = pltpu.roll(lv, 1, 1), pltpu.roll(lv, last, 1)
        west = jnp.where(index == 0, pltpu.roll(prev, 1, 1), here_up)
        east = jnp.where(index == last, pltpu.roll(follow, last, 1), here_down)
        others = (
            (lev[zi - 1, at : at + 8, cols] + lev[zi + 1, at : at + 8, cols])
            + (lev[zi, at - 1 : at + 7, cols] + lev[zi, at + 1 : at + 9, cols])
            + (west + east)
        )
        return lv, img[zi, at : at + 8, cols], others

    return local


LEV, IMG, HEA, READY, NEAR_LEV, NEAR_IMG, HELD = 0, 1, 2, 13, 14, 15, 16
CORNERS, READY_SEM = 13, 18


def body(level_set, image):
    zl, yl, length = level_set.shape
    shape = level_set.shape
    r = RADIUS
    both = jnp.stack([level_set, image])
    y_up, y_down = neighbours("row")
    z_up, z_down = neighbours("col")

    y_before = lax.ppermute(both[:, :, yl - r :, :].transpose(0, 2, 1, 3), "row", y_up)
    y_after = lax.ppermute(both[:, :, :r, :].transpose(0, 2, 1, 3), "row", y_down)
    z_before = lax.ppermute(both[:, zl - r :], "col", z_up)
    z_after = lax.ppermute(both[:, :r], "col", z_down)

    y_rows = np.arange(yl)
    wx1 = band(np.arange(length), np.arange(length), length)
    wx = jnp.concatenate([wx1, wx1], axis=0)

    def doubled(out_pos, in_pos):
        w = band(out_pos, in_pos)
        return jnp.concatenate([w, w], axis=1)

    def full(z0, zn, y0, yn):
        return ((z0, zn), (y0, yn), (0, length))

    depth = PAIR * 4 + 2 * r
    near = depth - r
    inner = zl - 2 * EDGE
    chunk = zl // 6 if zl % 6 == 0 else zl // 3
    n_chunks = zl // chunk
    interior = dict(
        name="interior", rows=yl, rows_out=yl - 2 * EDGE, length=length, planes=zl,
        pair=PAIR, steps=inner // PAIR,
        base=lambda t: EDGE - r + PAIR * t, out_z=lambda t: EDGE + PAIR * t,
        groups=((EDGE, yl - 2 * EDGE, EDGE),), local_at=(LEV, IMG),
        copies=[
            (f, (), full(z, chunk, 0, yl), f, (), full(z, chunk, 0, yl))
            for z in range(0, zl, chunk) for f in (LEV, IMG)
        ],
        fills=[
            (
                (2 * c, 2 * c + 1),
                (2 * c + 4, 2 * c + 5) if c + 2 < n_chunks else (),
                None, (c * chunk, (c + 1) * chunk), ((0, yl, True),),
            )
            for c in range(n_chunks)
        ],
        first=range(4),
        h_export=((0, near), (zl - near, near)),
        z_export=(0, yl - TILE, yl, 2 * yl - TILE),
        late_waits=(),
        extra_out=[
            jax.ShapeDtypeStruct(shape, jnp.float32),
            jax.ShapeDtypeStruct((inner, 4 * TILE, 4 * length), jnp.bfloat16),
        ],
    )
    out, hea, near_rows = run_part(
        interior, shape, [level_set, image],
        doubled(y_rows[EDGE : yl - EDGE], y_rows), wx, None,
    )

    edge_last = jnp.stack([y_before[:, :, zl - r :], y_after[:, :, zl - r :]])
    edge_first = jnp.stack([y_before[:, :, :r], y_after[:, :, :r]])
    corner_before = lax.ppermute(edge_last.transpose(0, 1, 3, 2, 4), "col", z_up)
    corner_after = lax.ppermute(edge_first.transpose(0, 1, 3, 2, 4), "col", z_down)

    half = EDGE + TILE
    z_lo, z_n = EDGE - r, zl - 2 * (EDGE - r)
    halo = ((0, r), (0, zl), (0, length))
    copies = [(2 + side, (f,), halo, HELD, (side, f), halo) for side in range(2) for f in range(2)]
    n_first = len(copies)
    for f, dst in ((0, NEAR_LEV), (1, NEAR_IMG)):
        copies += [
            (f, (), full(z_lo, z_n, 0, TILE), dst, (), full(z_lo, z_n, EDGE, TILE)),
            (f, (), full(z_lo, z_n, yl - TILE, TILE), dst, (), full(z_lo, z_n, half, TILE)),
        ]
    y_edges = dict(
        name="y_edges", rows=2 * EDGE, rows_out=2 * EDGE, length=length, planes=zl,
        pair=2 * PAIR, steps=inner // (2 * PAIR),
        base=lambda t: EDGE - r + 2 * PAIR * t, out_z=lambda t: EDGE + 2 * PAIR * t,
        first=range(n_first),
        groups=((EDGE, EDGE, 0), (half + EDGE, EDGE, yl - EDGE)),
        local_at=(NEAR_LEV, NEAR_IMG),
        copies=copies,
        fills=[((), (), None, (z_lo, z_lo + z_n), ((0, 2 * EDGE, True),))],
        h_export=(), z_export=(), late_waits=tuple(range(n_first, len(copies))),
        extra_out=[
            jax.ShapeDtypeStruct((2, 2, length // LANES, zl * EDGE, LANES), jnp.float32)
        ],
        ready=4 * TILE, ready_src=4, strip_waits=tuple(range(n_first)),
    )
    out_pos = np.concatenate([y_rows[:EDGE], y_rows[yl - EDGE :]])
    halo_pos = np.concatenate([np.arange(-EDGE, 0), np.arange(yl, yl + EDGE)])
    near_pos = np.concatenate([np.arange(TILE), np.arange(yl - TILE, yl)])
    out, y_strips = run_part(
        y_edges, shape, [level_set, image, y_before, y_after, near_rows],
        jnp.concatenate([doubled(out_pos, halo_pos), doubled(out_pos, near_pos)], axis=1),
        wx, out,
    )
    y_strips = y_strips.reshape(2, 2, length // LANES, zl, EDGE, LANES)

    rows = yl + 2 * EDGE
    copies, waits = [], []
    ring = ((0, 2), (0, 2), (0, r), (0, r), (0, length))
    for side, (z_dst, src, dst) in enumerate(((0, 0, r), (depth + near, zl - near, depth))):
        n_before = len(copies)
        copies.append((3 + side, (), ring, CORNERS, (side,), ring))
        copies += [
            (5 + side, (f,), full(0, r, 0, yl), f, (), full(z_dst, r, EDGE, yl))
            for f in (LEV, IMG)
        ]
        n_halo = len(copies)
        copies.append((7, (), full(src, near, 0, yl), HEA, (), full(dst, near, EDGE, yl)))
        for f in (LEV, IMG):
            copies.append((f, (), full(src, near, 0, yl), f, (), full(dst, near, EDGE, yl)))
            copies += [
                (
                    2, (t, f, lane // LANES), ((src, near), (0, EDGE), (0, LANES)),
                    f, (), ((dst, near), (row, EDGE), (lane, LANES)),
                )
                for t, row in ((0, 0), (1, EDGE + yl))
                for lane in range(0, length, LANES)
            ]
        waits.append((tuple(range(n_before, n_halo)), tuple(range(n_halo, len(copies)))))
    whole = ((0, rows, True),)
    inside = ((0, EDGE, True), (EDGE, yl, False), (EDGE + yl, EDGE, True))
    side_steps = EDGE // PAIR
    z_edges = dict(
        name="z_edges", rows=rows, rows_out=yl, length=length, planes=2 * depth,
        pair=PAIR, steps=2 * side_steps,
        base=lambda t: depth * (t // side_steps) + PAIR * (t % side_steps),
        out_z=lambda t: (zl - EDGE) * (t // side_steps) + PAIR * (t % side_steps),
        groups=((EDGE, yl, 0),), local_at=(LEV, IMG),
        copies=copies,
        first=waits[0][0] + waits[0][1],
        fills=[
            (waits[0][0], (), 0, (0, r), whole),
            (waits[0][1], waits[1][0] + waits[1][1], None, (r, depth), inside),
        ],
        late_fills=(
            side_steps // 2 - 1,
            [
                (waits[1][0], (), 1, (depth + near, 2 * depth), whole),
                (waits[1][1], (), None, (depth, depth + near), inside),
            ],
        ),
        corners=(0, depth + near),
        h_export=(), z_export=(), late_waits=(), extra_out=[],
    )
    (out,) = run_part(
        z_edges, shape,
        [level_set, image, y_strips, corner_before, corner_after, z_before, z_after, hea],
        doubled(y_rows, np.arange(-EDGE, yl + EDGE)), wx, out,
    )
    return out


def solution(mesh):
    return jax.shard_map(
        body,
        mesh=mesh,
        in_specs=(P("col", "row", None), P("col", "row", None)),
        out_specs=P("col", "row", None),
        check_vma=False,
    )
```
